32 devices in a mesh: lat: 4 (over y, x), lon: 8 (over z, core).
Axes of the slice: x: 2, y: 2, z: 4, core: 2. Of those that a mesh axis runs over, the one named last changes fastest.
Arguments:
- tracer: float32 [1152, 512, 128], P('lon', 'lat'), may hold values from -6 to 6
- courant: float32 [2, 1152, 512, 128], P(None, 'lon', 'lat'), may hold values from -0.45 to 0.45
- polar_mask: int32 [512], replicated, may hold values from 0 to 1, as said below
- cutoff: int32 [512], replicated, may hold values from 2 to 576
Outputs:
- advected: float32 [1152, 512, 128], P('lon', 'lat')
The draws below stay inside these ranges and needn't reach their ends.
Inputs may be any that keep to these rules, and one draw needn't show every extreme that they name: polar_mask is 1 on the first a rows and on the last b rows, with a and b each between 64 and 256, and 0 on all other rows.
All inputs are finite; a program needn't handle non-finite values.
Results may differ from the reference program's by a relative error of at most 0.00007.
Values sent between devices are 32-bit elements; how exact they have to be, the bound alone decides.
A program may use at most 256 MiB of HBM per device.

```python
import jax
import jax.numpy as jnp
from jax import lax

NLON = 1152
CLAT = 128
NF = 128
NLAT = 512


def draw_polar_mask(key, part):
    north_depth = jax.random.randint(jax.random.fold_in(key, 101), (), CLAT // 2, 2 * CLAT + 1)
    south_depth = jax.random.randint(jax.random.fold_in(key, 202), (), CLAT // 2, 2 * CLAT + 1)
    rows = jnp.arange(NLAT, dtype=jnp.int32)
    north = rows < north_depth
    south = rows >= NLAT - south_depth
    return jnp.where(north | south, 1, 0).astype(jnp.int32)


def place_ends(values, rng, least, top_value):
    longest = values.shape.index(max(values.shape))
    spots = []
    for shift in (0, 1):
        where = [jax.random.randint(jax.random.fold_in(rng, axis), (), 0, length) for axis, length in enumerate(values.shape)]
        where[longest] = (where[longest] + shift) % values.shape[longest]
        spots.append(tuple(where))
    return values.at[spots[0]].set(least).at[spots[1]].set(top_value)


def level_of(rng, dims, pieces, least, top_value):
    loudness = 1.0
    for position, blocks in pieces:
        heights = jax.random.uniform(jax.random.fold_in(jax.random.fold_in(rng, 6), position), (blocks,), jnp.float32, least / len(pieces), top_value / len(pieces))
        loudness = loudness * jnp.repeat(jnp.exp(heights), dims[position] // blocks).reshape((-1,) + (1,) * (len(dims) - 1 - position))
    return loudness


def normal_values(key, dims, spread, bound, shards=(), kind=jnp.bfloat16):
    entries = spread * jax.random.normal(key, dims, jnp.float32)
    if shards:
        entries = entries * level_of(key, dims, shards, -0.22, 0.18)
    return jnp.clip(entries, -bound, bound).astype(kind)


def setup_inputs(seed: int = 0) -> dict:
    key_list = jax.random.split(jax.random.key(seed), 5)
    return {
        "tracer": normal_values(key_list[0], (NLON, NLAT, NF), 1.0, 6.0, ((0, 8), (1, 4)), jnp.float32),
        "courant": jnp.clip(jax.random.uniform(key_list[1], (2, NLON, NLAT, NF), jnp.float32, -0.45, 0.45) * level_of(key_list[1], (2, NLON, NLAT, NF), ((1, 8), (2, 4)), -0.4, 0.0), -0.45, 0.45),
        "polar_mask": draw_polar_mask(jax.random.fold_in(key_list[4], 71), 0),
        "cutoff": place_ends(jax.random.randint(key_list[3], (NLAT,), 2, NLON // 2 + 1), jax.random.fold_in(key_list[3], 1), 2, (NLON // 2 + 1) - 1).astype(jnp.int32),
    }


def flux_change(padded_field, padded_speed, axis, count):
    def part(array, first):
        return lax.slice_in_dim(array, first, first + count + 1, axis=axis)
    far_low = part(padded_field, 0)
    low = part(padded_field, 1)
    high = part(padded_field, 2)
    far_high = part(padded_field, 3)
    speed = part(padded_speed, 2)
    face = (7.0 / 12.0) * (low + high) - (1.0 / 12.0) * (far_low + far_high)
    limited = jnp.clip(face, jnp.minimum(low, high), jnp.maximum(low, high))
    flux = speed * limited
    return lax.slice_in_dim(flux, 1, count + 1, axis=axis) - lax.slice_in_dim(flux, 0, count, axis=axis)


def reference(tracer, courant, polar_mask, cutoff):
    nlon, nlat, nf = tracer.shape
    blocks = 8
    width = nf // blocks

    def one_block(items):
        field, speed_x, speed_y = items
        spectrum = jnp.fft.rfft(field, axis=0)
        keep = (jnp.arange(nlon // 2 + 1, dtype=jnp.int32)[:, None] < cutoff[None, :]).astype(field.dtype)
        smooth = jnp.fft.irfft(spectrum * keep[:, :, None], n=nlon, axis=0).astype(field.dtype)
        weight = polar_mask.astype(field.dtype)[None, :, None]
        filtered = field + weight * (smooth - field)
        wide_field = jnp.pad(filtered, ((2, 2), (0, 0), (0, 0)), mode="wrap")
        wide_speed = jnp.pad(speed_x, ((2, 2), (0, 0), (0, 0)), mode="wrap")
        tall_field = jnp.pad(filtered, ((0, 0), (2, 2), (0, 0)))
        tall_speed = jnp.pad(speed_y, ((0, 0), (2, 2), (0, 0)))
        change_x = flux_change(wide_field, wide_speed, 0, nlon)
        change_y = flux_change(tall_field, tall_speed, 1, nlat)
        return filtered - change_x - change_y

    def split(array):
        return array.reshape(nlon, nlat, blocks, width).transpose(2, 0, 1, 3)

    result = lax.map(one_block, (split(tracer), split(courant[0]), split(courant[1])))
    return result.transpose(1, 2, 0, 3).reshape(nlon, nlat, nf)
```

```python
import functools
import math

import jax
import jax.numpy as jnp
import ml_dtypes
import numpy as np
from jax import lax
from jax.experimental import pallas as pl
from jax.experimental.pallas import tpu as pltpu
from jax.sharding import PartitionSpec as P

MESH = pl.DeviceIdType.MESH


def halves(table):
    high = table.astype(ml_dtypes.bfloat16)
    low = (table - high.astype(np.float64)).astype(ml_dtypes.bfloat16)
    return high, low


def hartley_tables(nlon):
    half = nlon // 2
    u = np.arange(half, dtype=np.int64)
    even = (u[:, None] * u[None, :]) % half * (2.0 * math.pi / half)
    odd = ((2 * u[:, None] + 1) * (2 * u[None, :] + 1)) % (2 * nlon) * (math.pi / nlon)
    cas = lambda t: np.cos(t) + np.sin(t)
    return (*halves(cas(even)), *halves(cas(odd)))


def split(x):
    high = x.astype(jnp.bfloat16)
    return high, (x - high.astype(jnp.float32)).astype(jnp.bfloat16)


def times(high, low, x):
    x_high, x_low = split(x)
    dot = functools.partial(jnp.dot, preferred_element_type=jnp.float32)
    return dot(high[...], x_high) + (dot(low[...], x_high) + dot(high[...], x_low))


def filter_kernel(devices, bands, chunks, mask_ref, cut_ref, tracer, courant, *rest):
    tables, rest = rest[:4], rest[4:]
    (out, before, after, edge_x, edge_y, ring, even_h, even_l, odd_h, odd_l,
     table_sem, send_a, recv_a, self_a, send_b, recv_b, self_b, send_e, recv_e) = rest
    me, lat = lax.axis_index("lon"), lax.axis_index("lat")
    clon, clat, nf = tracer.shape
    size = clat // devices // chunks
    nlon = clon * devices
    half = nlon // 2
    order = sorted(range(1, devices), key=lambda off: -min(off, devices - off))
    peers = [lax.rem(me + off, devices) for off in order]
    west = lax.rem(me + devices - 1, devices)
    north, south = lax.rem(lat + bands - 1, bands), lax.rem(lat + 1, bands)

    loads = [
        pltpu.make_async_copy(table, place, table_sem.at[i])
        for i, (table, place) in enumerate(zip(tables, (even_h, even_l, odd_h, odd_l)))
    ]
    for copy in loads:
        copy.start()

    barrier = pltpu.get_barrier_semaphore()
    for peer in peers:
        pl.semaphore_signal(barrier, inc=1, device_id={"lon": peer}, device_id_type=MESH)
    for band in (north, south):
        pl.semaphore_signal(barrier, inc=1, device_id={"lat": band}, device_id_type=MESH)
    pl.semaphore_wait(barrier, devices + 1)

    def first(owner, c):
        flip = owner // (devices // 2)
        tile = owner * chunks + c + flip * (chunks - 1 - 2 * c)
        return pl.multiple_of(tile * size, size)

    def landing(c):
        return ring.at[c, pl.ds(2 + me * clon, clon)]

    def result(owner, c):
        return ring.at[c, pl.ds(owner * clon, clon + 4)]

    def home(c):
        return out.at[:, pl.ds(first(me, c), size), :]

    def source(owner, c):
        return tracer.at[:, pl.ds(first(owner, c), size), :]

    there, back = [], []
    for c in range(chunks):
        own = pltpu.make_async_copy(source(me, c), landing(c), self_a.at[c])
        sent = [
            pltpu.make_async_remote_copy(
                source(peer, c), landing(c), send_a.at[c, j], recv_a.at[c, j],
                device_id={"lon": peer}, device_id_type=MESH)
            for j, peer in enumerate(peers)
        ]
        own.start()
        for copy in sent:
            copy.start()
        there.append((own, sent))

    def edge(src, dst, k, device):
        return pltpu.make_async_remote_copy(
            src, dst, send_e.at[k], recv_e.at[k], device_id=device, device_id_type=MESH)

    def inner(ref, start):
        return ref.at[pl.ds(2, clon), pl.ds(start, 8), :]

    go_x = edge(courant.at[0, pl.ds(0, 1)], edge_x, 0, {"lon": west})
    go_y = edge(courant.at[1, :, pl.ds(0, 8), :], edge_y, 1, {"lat": north})
    go_north = edge(inner(out, 0), after, 2, {"lat": north})
    go_south = edge(inner(out, clat - 8), before, 3, {"lat": south})
    go_x.start()
    go_y.start()
    for copy in loads:
        copy.wait()

    lane = lax.broadcasted_iota(jnp.int32, (1, 2 * nf), 1)
    index = lax.broadcasted_iota(jnp.int32, (half, 2 * nf), 0)
    scale = 1.0 / nlon

    for c in range(chunks):
        own, sent = there[c]
        own.wait()
        for copy in sent:
            copy.wait_recv()
        flat = ring.at[c].reshape((nlon + 4) * size, nf)
        first_row = lat * clat + first(me, c)

        def pair(p, carry):
            def block(start, count, r):
                return (pl.ds(start * size + r, count, stride=size), slice(None))

            def load(start):
                return jnp.concatenate(
                    [flat[block(start, half, 2 * p + s)] for s in range(2)], axis=1)

            row = first_row + 2 * p
            cut = jnp.where(lane < nf, cut_ref[row], cut_ref[row + 1])
            mask = jnp.where(lane < nf, mask_ref[row], mask_ref[row + 1])
            low, high = load(2), load(2 + half)
            even = times(even_h, even_l, low + high)
            odd = times(odd_h, odd_l, low - high)
            wave = 2 * index
            even = jnp.where(jnp.minimum(wave, nlon - wave) < cut, even * scale, 0.0)
            odd = jnp.where(jnp.minimum(wave + 1, nlon - 1 - wave) < cut, odd * scale, 0.0)
            even = times(even_h, even_l, even)
            odd = times(odd_h, odd_l, odd)
            low = jnp.where(mask > 0, even + odd, low)
            high = jnp.where(mask > 0, even - odd, high)
            for s in range(2):
                r = 2 * p + s
                lo, hi = low[:, s * nf:(s + 1) * nf], high[:, s * nf:(s + 1) * nf]
                flat[block(2, half, r)] = lo
                flat[block(2 + half, half, r)] = hi
                for e in range(2):
                    flat[pl.ds((2 + nlon + e) * size + r, 1), :] = lo[e:e + 1]
                    flat[pl.ds(e * size + r, 1), :] = hi[half - 2 + e:half - 1 + e]
            return carry

        lax.fori_loop(0, size // 2, pair, 0)

        own = pltpu.make_async_copy(result(me, c), home(c), self_b.at[c])
        sent = [
            pltpu.make_async_remote_copy(
                result(peer, c), home(c), send_b.at[c, j], recv_b.at[c, j],
                device_id={"lon": peer}, device_id_type=MESH)
            for j, peer in enumerate(peers)
        ]
        own.start()
        for copy in sent:
            copy.start()
        back.append((own, sent))

    for own, sent in there:
        for copy in sent:
            copy.wait_send()
    go_x.wait()
    for c in range(chunks):
        own, sent = back[c]
        own.wait()
        for copy in sent:
            copy.wait()
        if c == 0:
            @pl.when(lat > 0)
            def _():
                go_north.start()

            @pl.when(lat < bands - 1)
            def _():
                go_south.start()
    go_y.wait()

    @pl.when(lat > 0)
    def _():
        go_north.wait_send()
        go_south.wait_recv()

    @pl.when(lat < bands - 1)
    def _():
        go_south.wait_send()
        go_north.wait_recv()


def by_kernel(tracer, courant, polar_mask, cutoff, devices, bands):
    clon, clat, nf = tracer.shape
    nlon = clon * devices
    half = nlon // 2
    chunks = clat // devices // 8
    tables = [jnp.asarray(t) for t in hartley_tables(nlon)]
    smem = pl.BlockSpec(memory_space=pltpu.SMEM)
    hbm = pl.BlockSpec(memory_space=pltpu.HBM)
    dma = pltpu.SemaphoreType.DMA
    pairs, alone = dma((chunks, devices - 1)), dma((chunks,))
    shape = lambda *dims: jax.ShapeDtypeStruct(dims, jnp.float32)
    edge = shape(clon, 8, nf)
    return pl.pallas_call(
        functools.partial(filter_kernel, devices, bands, chunks),
        out_shape=(shape(clon + 4, clat, nf), edge, edge, shape(1, clat, nf), edge),
        in_specs=[smem, smem] + [hbm] * 6,
        out_specs=(hbm,) * 5,
        scratch_shapes=[pltpu.VMEM((chunks, nlon + 4, 8, nf), jnp.float32)]
        + [pltpu.VMEM((half, half), jnp.bfloat16)] * 4
        + [dma((4,)), pairs, pairs, alone, pairs, pairs, alone, dma((4,)), dma((4,))],
        compiler_params=pltpu.CompilerParams(
            collective_id=0, has_side_effects=True, vmem_limit_bytes=65000 << 10),
        name="filter_exchange",
    )(polar_mask, cutoff, tracer, courant, *tables)


def limited(far_low, low, high, far_high):
    face = (7.0 / 12.0) * (low + high) - (1.0 / 12.0) * (far_low + far_high)
    return jnp.minimum(jnp.maximum(face, jnp.minimum(low, high)), jnp.maximum(low, high))


def flux_kernel(bands, field, speed_x, next_x, edge_x, speed_y, edge_y, before, after, out, tall, flux):
    count, clat = out.shape[0], out.shape[1]
    final = pl.program_id(0) == pl.num_programs(0) - 1
    lat = lax.axis_index("lat")
    top, bottom = lat > 0, lat < bands - 1

    def flux_x(i, speed):
        return speed * limited(field[i], field[i + 1], field[i + 2], field[i + 3])

    def column(c, low_flux, speed):
        high_flux = flux_x(c + 1, speed)
        value = field[c + 2]
        tall[8:8 + clat] = value
        tall[0:8] = jnp.where(top, before[c], 0.0)
        tall[8 + clat:16 + clat] = jnp.where(bottom, after[c], 0.0)
        flux[0:clat] = speed_y[c] * limited(
            tall[6:6 + clat], tall[7:7 + clat], value, tall[9:9 + clat])
        flux[clat:clat + 1] = jnp.where(bottom, edge_y[c, 0:1], 0.0) * limited(
            tall[6 + clat:7 + clat], tall[7 + clat:8 + clat],
            tall[8 + clat:9 + clat], tall[9 + clat:10 + clat])
        out[c] = value - (high_flux - low_flux) - (flux[1:clat + 1] - flux[0:clat])
        return high_flux

    carry = flux_x(0, speed_x[0])
    carry = lax.fori_loop(0, count - 1, lambda c, low: column(c, low, speed_x[c + 1]), carry)
    column(count - 1, carry, jnp.where(final, edge_x[0], next_x[0]))


def advect(field, before, after, edge_x, edge_y, courant, bands):
    _, clon, clat, nf = courant.shape
    block = math.gcd(clon, 16)
    squeezed = pl.Squeezed()
    return pl.pallas_call(
        functools.partial(flux_kernel, bands),
        grid=(clon // block,),
        out_shape=jax.ShapeDtypeStruct((clon, clat, nf), jnp.float32),
        in_specs=[
            pl.BlockSpec((pl.Element(block + 4), pl.Element(clat), pl.Element(nf)),
                         lambda i: (i * block, 0, 0)),
            pl.BlockSpec((squeezed, block, clat, nf), lambda i: (0, i, 0, 0)),
            pl.BlockSpec((squeezed, 1, clat, nf),
                         lambda i: (0, jnp.minimum((i + 1) * block, clon - 1), 0, 0)),
            pl.BlockSpec((1, clat, nf), lambda i: (0, 0, 0)),
            pl.BlockSpec((squeezed, block, clat, nf), lambda i: (1, i, 0, 0)),
            pl.BlockSpec((block, 8, nf), lambda i: (i, 0, 0)),
            pl.BlockSpec((block, 8, nf), lambda i: (i, 0, 0)),
            pl.BlockSpec((block, 8, nf), lambda i: (i, 0, 0)),
        ],
        out_specs=pl.BlockSpec((block, clat, nf), lambda i: (i, 0, 0)),
        scratch_shapes=[pltpu.VMEM((clat + 16, nf), jnp.float32),
                        pltpu.VMEM((clat + 8, nf), jnp.float32)],
        compiler_params=pltpu.CompilerParams(vmem_limit_bytes=65000 << 10),
        name="flux_step",
    )(field, courant, courant, edge_x, courant, edge_y, before, after)


def by_collectives(tracer, courant, polar_mask, cutoff, devices, bands):
    clon, clat, nf = tracer.shape
    nlon, half = clon * devices, clon * devices // 2
    circles = lax.all_to_all(tracer, "lon", split_axis=1, concat_axis=0, tiled=True)
    rows = clat // devices
    start = lax.axis_index("lat") * clat + lax.axis_index("lon") * rows
    mask = lax.dynamic_slice_in_dim(polar_mask, start, rows)[None, :, None]
    cut = lax.dynamic_slice_in_dim(cutoff, start, rows)[None, :, None]
    tables = [jnp.asarray(t).astype(jnp.float32) for t in hartley_tables(nlon)]
    apply = lambda h, l, x: jnp.einsum("uk,krc->urc", h + l, x, precision=lax.Precision.HIGHEST)
    low, high = circles[:half], circles[half:]
    wave = 2 * lax.broadcasted_iota(jnp.int32, (half, 1, 1), 0)
    even = apply(tables[0], tables[1], low + high) * (1.0 / nlon)
    odd = apply(tables[2], tables[3], low - high) * (1.0 / nlon)
    even = jnp.where(jnp.minimum(wave, nlon - wave) < cut, even, 0.0)
    odd = jnp.where(jnp.minimum(wave + 1, nlon - 1 - wave) < cut, odd, 0.0)
    even = apply(tables[0], tables[1], even)
    odd = apply(tables[2], tables[3], odd)
    smooth = jnp.concatenate([even + odd, even - odd], axis=0)
    done = jnp.where(mask > 0, smooth, circles)
    field = lax.all_to_all(done, "lon", split_axis=0, concat_axis=1, tiled=True)
    up = [(i, (i + 1) % devices) for i in range(devices)]
    down = [(j, i) for i, j in up]
    before = lax.ppermute(field[clon - 2:], "lon", up)
    after = lax.ppermute(field[:2], "lon", down)
    wide = jnp.concatenate([before, field, after], axis=0)
    south = [(i, i + 1) for i in range(bands - 1)]
    north = [(j, i) for i, j in south]
    edge_x = lax.ppermute(courant[0, :1], "lon", down)
    edge_y = lax.ppermute(courant[1, :, :8], "lat", north)
    before = lax.ppermute(field[:, clat - 8:], "lat", south)
    after = lax.ppermute(field[:, :8], "lat", north)
    return wide, before, after, edge_x, edge_y


ROWS_AT_EDGE = 2
SKEW = 2
LIMITS = (40, 48, 56, 62, 66, 70, 74, 80, 88)


def basis(nlon):
    half = nlon // 2
    i, n = np.arange(half), np.arange(nlon)
    tables = []
    for wave, sine in (((i + 1) // 2, (i % 2 == 0) & (i > 0)), (half - (i + 1) // 2, (i % 2 == 0) & (i > 0))):
        angle = (wave[:, None] * n[None, :]) % nlon * (2.0 * math.pi / nlon)
        size = np.where((wave == 0) | (wave == half), 1.0, 2.0) / nlon
        tables.append(np.where(sine[:, None], np.sin(angle), np.cos(angle)) * np.sqrt(size)[:, None])
    return np.stack(tables)


def forward_tables(nlon, devices):
    half, clon = nlon // 2, nlon // devices
    whole = basis(nlon).reshape(2, half, devices, clon).transpose(2, 0, 1, 3)
    high, low = halves(whole)
    return np.concatenate([high, low, high], axis=-1)


def inverse_tables(nlon, devices):
    half, clon = nlon // 2, nlon // devices
    blocks = -(-half // 128)
    rows = -(-(clon + 4) // 8) * 8
    whole = np.zeros((2, blocks * 128, nlon))
    whole[:, :half] = basis(nlon)
    place = (np.arange(devices)[:, None] * clon + np.arange(rows)[None, :] - 2) % nlon
    whole = whole[:, :, place].reshape(2, blocks, 128, devices, rows).transpose(3, 0, 4, 1, 2)
    high, low = halves(whole)
    return np.stack([high, low, high], axis=-2).reshape(devices, 2, rows, blocks * 384)


def kept(cut, half):
    low = 2 * cut - 1 <= half
    count = jnp.where(low, 2 * cut - 1, 2 * half + 1 - 2 * cut)
    return low, count, (count + 7) // 8 * 8


def forward_kernel(mask_ref, cut_ref, tracer, tables, packed, x, table, out, x_sem, table_sem, out_sem):
    me, lat = lax.axis_index("lon"), lax.axis_index("lat")
    clon, clat, nf = tracer.shape
    half = table.shape[1]
    parts = x_sem.shape[0]
    step = clat // parts
    load = pltpu.make_async_copy(tables.at[me], table, table_sem)
    load.start()
    order = [0, parts - 1] + list(range(1, parts - 1))
    reads = [
        pltpu.make_async_copy(
            tracer.at[:, pl.ds(p * step, step), :], x.at[:, pl.ds(p * step, step), :], x_sem.at[p])
        for p in range(parts)
    ]
    for p in order:
        reads[p].start()
    flat = x.reshape(clon * clat, nf)

    def row_step(row, place):
        low, count, padded = kept(cut_ref[lat * clat + row], half)
        polar = mask_ref[lat * clat + row] > 0
        which = jnp.where(low, 0, 1)

        @pl.when(polar)
        def _():
            high, rest = split(flat[pl.ds(row, clon, stride=clat), :])
            stack = jnp.concatenate([high, high, rest], axis=0)
            blocks = -(-half // 128)
            for b in range(1, blocks + 1):
                top = min(b * 128, half)

                @pl.when((padded > (b - 1) * 128) & (padded <= top))
                def _(top=top):
                    out[pl.ds(place, top), :] = jnp.dot(
                        table[which, 0:top], stack, preferred_element_type=jnp.float32)

        return jnp.where(polar, padded, 0)

    def write(c):
        at = pl.ds(pl.multiple_of(c * half, 8), half)
        return pltpu.make_async_copy(out.at[at], packed.at[at], out_sem.at[c])

    load.wait()
    reads[0].wait()
    reads[parts - 1].wait()
    for i in range(ROWS_AT_EDGE):
        row_step(i, i * half)
        row_step(clat - ROWS_AT_EDGE + i, (ROWS_AT_EDGE + i) * half)
    for i in range(2 * ROWS_AT_EDGE):
        write(i).start()
    for p in range(1, parts - 1):
        reads[p].wait()

    def body(row, carry):
        place, done = carry
        place = place + row_step(row, pl.multiple_of(place, 8))
        full = (done + 1) * half <= place

        @pl.when(full)
        def _():
            write(done).start()

        return place, done + jnp.where(full, 1, 0)

    place, done = lax.fori_loop(
        ROWS_AT_EDGE, clat - ROWS_AT_EDGE, body, (2 * ROWS_AT_EDGE * half, 2 * ROWS_AT_EDGE))
    tail = done * half < place

    @pl.when(tail)
    def _():
        write(done).start()

    done = done + jnp.where(tail, 1, 0)

    @pl.loop(0, done)
    def _(c):
        write(c).wait()


def exchange_kernel(bands, packed, tracer, courant, totals, lon_low, lon_high, lat_low, lat_high, edge_x, edge_y,
                    own, mate, first, second, own_sem, mate_send, mate_recv, first_send, first_recv,
                    second_send, second_recv, home_sem, home_send, home_recv, band_send, band_recv,
                    edge_send, edge_recv):
    me, lat = lax.axis_index("lon"), lax.axis_index("lat")
    clon, clat, nf = tracer.shape
    n, chunk = own.shape[0], own.shape[1]
    half = 2 * chunk
    base = 2 * ROWS_AT_EDGE * half
    devices = 8
    z, core = me // 2, me % 2
    other = me + 1 - 2 * core
    outer = (z == 0) | (z == 3)
    inner = jnp.logical_not(outer)
    inward = lax.rem(jnp.where(z < 2, me + 2, me + devices - 2), devices)
    outward = lax.rem(jnp.where(z < 2, me + devices - 2, me + 2), devices)
    east, west = lax.rem(me + 1, devices), lax.rem(me + devices - 1, devices)
    north, south = lax.rem(lat + bands - 1, bands), lax.rem(lat + 1, bands)

    barrier = pltpu.get_barrier_semaphore()
    for peer in (other, inward, outward, east, west):
        pl.semaphore_signal(barrier, inc=1, device_id={"lon": peer}, device_id_type=MESH)
    for band in (north, south):
        for peer in (me, other):
            pl.semaphore_signal(barrier, inc=1, device_id={"lat": band, "lon": peer}, device_id_type=MESH)
    pl.semaphore_wait(barrier, 9)

    def part(c, which):
        return pl.ds(pl.multiple_of((2 * c + which) * chunk, 8), chunk)

    def remote(src, dst, send, recv, **device):
        return pltpu.make_async_remote_copy(src, dst, send, recv, device_id=device, device_id_type=MESH)

    def to_own(c):
        return pltpu.make_async_copy(packed.at[part(c, core)], own.at[c], own_sem.at[c])

    def to_mate(c):
        return remote(packed.at[part(c, 1 - core)], mate.at[c], mate_send.at[c], mate_recv.at[c], lon=other)

    def out_first(c):
        return remote(own.at[c], first.at[c], first_send.at[c], first_recv.at[c], lon=inward)

    def in_second(c):
        return remote(first.at[c], second.at[c], first_send.at[c], second_recv.at[c], lon=inward)

    def out_second(c):
        return remote(second.at[c], second.at[c], second_send.at[c], second_recv.at[c], lon=outward)

    def home(src, c):
        place = totals.at[pl.ds(pl.multiple_of(base + (2 * c + core) * chunk, 8), chunk)]
        return (pltpu.make_async_copy(src.at[c], place, home_sem.at[c]),
                remote(src.at[c], place, home_send.at[c], home_recv.at[c], lon=other))

    def bands_of(src, c):
        up = c < ROWS_AT_EDGE
        row = c + ROWS_AT_EDGE * (1 if up else -1)
        place = totals.at[pl.ds(pl.multiple_of(row * half + core * chunk, 8), chunk)]
        return [
            remote(src.at[c], place, band_send.at[c, q], band_recv.at[c, core],
                   lat=north if up else south, lon=peer)
            for q, peer in enumerate((me, other))
        ]

    def emit(src, c):
        for copy in home(src, c):
            copy.start()
        for k in range(2 * ROWS_AT_EDGE):
            @pl.when((c == k) & ((lat > 0) if k < ROWS_AT_EDGE else (lat < bands - 1)))
            def _(k=k):
                for copy in bands_of(src, k):
                    copy.start()

    @pl.loop(0, n)
    def _(c):
        to_own(c).start()
        to_mate(c).start()

    def edge(src, dst, k, **device):
        return remote(src, dst, edge_send.at[k], edge_recv.at[k], **device)

    go_west = [edge(courant.at[0, pl.ds(0, 1)], edge_x, 0, lon=west),
               edge(tracer.at[pl.ds(0, 2)], lon_high, 1, lon=west)]
    go_east = [edge(tracer.at[pl.ds(clon - 2, 2)], lon_low, 2, lon=east)]
    go_north = [edge(courant.at[1, :, pl.ds(0, 8), :], edge_y, 3, lat=north),
                edge(tracer.at[:, pl.ds(0, 8), :], lat_high, 4, lat=north)]
    go_south = [edge(tracer.at[:, pl.ds(clat - 8, 8), :], lat_low, 5, lat=south)]
    edges = go_west + go_east + go_north + go_south
    for copy in edges:
        copy.start()

    @pl.loop(0, n + 3 * SKEW)
    def _(i):
        @pl.when(i < n)
        def _():
            to_own(i).wait()
            to_mate(i).wait_recv()
            own[i] = own[i] + mate[i]

            @pl.when(outer)
            def _():
                out_first(i).start()

        @pl.when(inner & (i >= SKEW) & (i < n + SKEW))
        def _():
            c = i - SKEW
            out_first(c).wait_recv()
            first[c] = first[c] + own[c]
            in_second(c).start()

        @pl.when(inner & (i >= 2 * SKEW) & (i < n + 2 * SKEW))
        def _():
            c = i - 2 * SKEW
            in_second(c).wait_recv()
            late, mine = second[c], own[c]
            own[c] = first[c] + late
            second[c] = late + mine
            out_second(c).start()
            emit(own, c)

        @pl.when(outer & (i >= 3 * SKEW))
        def _():
            c = i - 3 * SKEW
            out_second(c).wait_recv()
            second[c] = second[c] + own[c]
            emit(second, c)

    @pl.loop(0, n)
    def _(c):
        to_mate(c).wait_send()
        out_first(c).wait_send()

        @pl.when(inner)
        def _():
            out_second(c).wait_send()

        here, away = home(own, c)
        here.wait()
        away.wait()

    for copy in edges:
        copy.wait()
    for k in range(2 * ROWS_AT_EDGE):
        up = k < ROWS_AT_EDGE

        @pl.when((lat > 0) if up else (lat < bands - 1))
        def _(k=k):
            for copy in bands_of(own, k):
                copy.wait_send()

        @pl.when((lat < bands - 1) if up else (lat > 0))
        def _(k=k):
            for which in range(2):
                remote(own.at[k], own.at[k], band_send.at[k, 0], band_recv.at[k, which],
                       lat=north, lon=me).wait_recv()


def finish_kernel(bands, mask_ref, cut_ref, totals, tracer, lon_low, lon_high, lat_low, lat_high, edge_x, edge_y,
                  courant, tables, out, field, speed_x, speed_y, low_y, ring, table, flux,
                  todo, load_sem, courant_sem, ring_sem, out_sem):
    me, lat = lax.axis_index("lon"), lax.axis_index("lat")
    clon, clat, nf = tracer.shape
    half = (clon * 8) // 2
    deep = ring.shape[0]
    tall = clat + 16
    top, bottom = lat > 0, lat < bands - 1
    block = clon // out_sem.shape[0]

    inside = pl.ds(2, clon)
    loads = [
        pltpu.make_async_copy(src, dst, load_sem.at[k])
        for k, (src, dst) in enumerate((
            (tables.at[me], table),
            (tracer, field.at[inside, pl.ds(8, clat), :]),
            (lon_low, field.at[pl.ds(0, 2), pl.ds(8, clat), :]),
            (lon_high, field.at[pl.ds(clon + 2, 2), pl.ds(8, clat), :]),
            (lat_low, field.at[inside, pl.ds(0, 8), :]),
            (lat_high, field.at[inside, pl.ds(8 + clat, 8), :]),
        ))
    ]
    for copy in loads:
        copy.start()

    def speeds(b):
        at = pl.ds(b * block, block)
        return (pltpu.make_async_copy(courant.at[0, at], speed_x.at[at], courant_sem.at[0, b]),
                pltpu.make_async_copy(courant.at[1, at], speed_y.at[at], courant_sem.at[1, b]))

    def note(entry, place):
        row = lat * clat + entry - ROWS_AT_EDGE
        valid = (row >= 0) & (row < bands * clat)
        row = jnp.clip(row, 0, bands * clat - 1)
        low, count, padded = kept(cut_ref[row], half)
        return valid & (mask_ref[row] > 0), low, count, padded

    def put(m, entry, place):
        polar, low, count, padded = note(entry, place)

        @pl.when(polar)
        def _():
            todo[0, m] = place
            todo[1, m] = entry + 8 - ROWS_AT_EDGE
            todo[2, m] = count
            todo[3, m] = jnp.where(low, 0, 1)

        return m + jnp.where(polar, 1, 0), jnp.where(polar, padded, 0)

    m = jnp.int32(0)
    base = 2 * ROWS_AT_EDGE * half
    for k in range(2 * ROWS_AT_EDGE):
        entry = k if k < ROWS_AT_EDGE else clat + k
        m, _ = put(m, entry, k * half)
    for k in range(2 * ROWS_AT_EDGE):
        entry = ROWS_AT_EDGE + k if k < ROWS_AT_EDGE else clat - ROWS_AT_EDGE + k
        m, _ = put(m, entry, base + k * half)

    def listed(entry, carry):
        m, place = carry
        m, more = put(m, entry, place)
        return m, place + more

    m, _ = lax.fori_loop(2 * ROWS_AT_EDGE, clat, listed, (m, jnp.int32(2 * base)))

    def fetch(k):
        slot = lax.rem(k, deep)
        return pltpu.make_async_copy(
            totals.at[pl.ds(pl.multiple_of(todo[0, k], 8), half)],
            ring.at[slot, pl.ds(0, half)], ring_sem.at[slot])

    for k in range(deep - 1):
        @pl.when(k < m)
        def _(k=k):
            fetch(k).start()
    for b in range(clon // block):
        for copy in speeds(b):
            copy.start()
    last = pltpu.make_async_copy(edge_x, speed_x.at[pl.ds(clon, 1)], load_sem.at[6])
    edge = pltpu.make_async_copy(edge_y, low_y, load_sem.at[7])
    last.start()
    edge.start()
    for copy in loads:
        copy.wait()

    zero = jnp.zeros((clon, 8, nf), jnp.float32)

    @pl.when(jnp.logical_not(top))
    def _():
        field[2:clon + 2, 0:8, :] = zero

    @pl.when(jnp.logical_not(bottom))
    def _():
        field[2:clon + 2, 8 + clat:16 + clat, :] = zero

    flat = field.reshape((clon + 4) * tall, nf)
    index = lax.broadcasted_iota(jnp.int32, (128, nf), 0)

    @pl.loop(0, m)
    def _(k):
        @pl.when(k + deep - 1 < m)
        def _():
            fetch(k + deep - 1).start()

        fetch(k).wait()
        slot = lax.rem(k, deep)
        row, count, which = todo[1, k], todo[2, k], todo[3, k]
        for blocks in range(1, -(-half // 128) + 1):
            @pl.when((count > (blocks - 1) * 128) & (count <= blocks * 128))
            def _(blocks=blocks):
                stack = []
                for b in range(blocks):
                    s = ring[slot, b * 128:(b + 1) * 128, :]
                    if b == blocks - 1:
                        s = jnp.where(index + b * 128 < count, s, 0.0)
                    high, low = split(s)
                    stack += [high, high, low]
                y = jnp.dot(table[which, :, 0:384 * blocks], jnp.concatenate(stack, axis=0),
                            preferred_element_type=jnp.float32)[0:clon + 4]
                at = pl.ds(row, clon + 4, stride=tall)
                flat[at, :] = jnp.where(which == 0, y, flat[at, :] - y)

    for b in range(clon // block):
        for copy in speeds(b):
            copy.wait()
    last.wait()
    edge.wait()

    def flux_x(i):
        f = lambda k: field[i + k, 8:8 + clat, :]
        return speed_x[i] * limited(f(0), f(1), f(2), f(3))

    def column(c, low_flux):
        high_flux = flux_x(c + 1)
        f = lambda start, count: field[c + 2, start:start + count, :]
        value = f(8, clat)
        flux[0:clat] = speed_y[c] * limited(f(6, clat), f(7, clat), value, f(9, clat))
        flux[clat:clat + 1] = jnp.where(bottom, low_y[c, 0:1], 0.0) * limited(
            f(6 + clat, 1), f(7 + clat, 1), f(8 + clat, 1), f(9 + clat, 1))
        field[c, 8:8 + clat, :] = value - (high_flux - low_flux) - (flux[1:clat + 1] - flux[0:clat])
        return high_flux

    def result(b):
        at = pl.ds(b * block, block)
        return pltpu.make_async_copy(field.at[at, pl.ds(8, clat), :], out.at[at], out_sem.at[b])

    def strip(b, carry):
        carry = lax.fori_loop(b * block, (b + 1) * block, column, carry)
        result(b).start()
        return carry

    lax.fori_loop(0, clon // block, strip, flux_x(0))
    for b in range(clon // block):
        result(b).wait()


def by_spectrum(tracer, courant, polar_mask, cutoff, chunks, devices, bands):
    clon, clat, nf = tracer.shape
    nlon = clon * devices
    half = nlon // 2
    most = LIMITS[-1]
    smem = pl.BlockSpec(memory_space=pltpu.SMEM)
    hbm = pl.BlockSpec(memory_space=pltpu.HBM)
    dma = pltpu.SemaphoreType.DMA
    shape = lambda *dims: jax.ShapeDtypeStruct(dims, jnp.float32)
    big = pltpu.CompilerParams(vmem_limit_bytes=65000 << 10)
    forward, inverse = forward_tables(nlon, devices), inverse_tables(nlon, devices)

    packed = pl.pallas_call(
        forward_kernel,
        out_shape=shape(most * half, nf),
        in_specs=[smem, smem, hbm, hbm],
        out_specs=hbm,
        scratch_shapes=[
            pltpu.VMEM((clon, clat, nf), jnp.float32), pltpu.VMEM(forward.shape[1:], jnp.bfloat16),
            pltpu.VMEM(((most + 1) * half, nf), jnp.float32),
            dma((8,)), dma, dma((most,))],
        compiler_params=big,
        name="forward",
    )(polar_mask, cutoff, tracer, jnp.asarray(forward))

    def exchange(n, which):
        chunk = half // 2
        buffer = pltpu.VMEM((n, chunk, nf), jnp.float32)

        def call(packed, tracer, courant):
            return pl.pallas_call(
                functools.partial(exchange_kernel, bands),
                out_shape=(shape((most + 2 * 2 * ROWS_AT_EDGE) * half, nf), shape(2, clat, nf), shape(2, clat, nf),
                           shape(clon, 8, nf), shape(clon, 8, nf), shape(1, clat, nf), shape(clon, 8, nf)),
                in_specs=[hbm] * 3,
                out_specs=(hbm,) * 7,
                scratch_shapes=[buffer] * 4 + [dma((n,))] * 10
                + [dma((2 * ROWS_AT_EDGE, 2)), dma((2 * ROWS_AT_EDGE, 2)), dma((6,)), dma((6,))],
                compiler_params=pltpu.CompilerParams(
                    collective_id=1 + which, has_side_effects=True, vmem_limit_bytes=65000 << 10),
                name=f"exchange_{n}",
            )(packed, tracer, courant)

        return call

    which = sum(jnp.where(chunks > limit, 1, 0) for limit in LIMITS[:-1])
    parts = lax.switch(which, [exchange(n, i) for i, n in enumerate(LIMITS)], packed, tracer, courant)

    blocks = -(-half // 128)
    return pl.pallas_call(
        functools.partial(finish_kernel, bands),
        out_shape=shape(clon, clat, nf),
        in_specs=[smem, smem] + [hbm] * 10,
        out_specs=hbm,
        scratch_shapes=[
            pltpu.VMEM((clon + 4, clat + 16, nf), jnp.float32),
            pltpu.VMEM((clon + 1, clat, nf), jnp.float32), pltpu.VMEM((clon, clat, nf), jnp.float32),
            pltpu.VMEM((clon, 8, nf), jnp.float32),
            pltpu.VMEM((4, blocks * 128, nf), jnp.float32), pltpu.VMEM(inverse.shape[1:], jnp.bfloat16),
            pltpu.VMEM((clat + 8, nf), jnp.float32),
            pltpu.SMEM((4, clat + 8), jnp.int32),
            dma((8,)), dma((2, 9)), dma((4,)), dma((9,))],
        compiler_params=big,
        name="finish",
    )(polar_mask, cutoff, parts[0], tracer, *parts[1:], courant, jnp.asarray(inverse))


def on_device(tracer, courant, polar_mask, cutoff):
    devices, bands = lax.axis_size("lon"), lax.axis_size("lat")
    clon, clat, _ = tracer.shape
    fits = clat % (8 * devices) == 0 and bands > 2

    def by_circles(tracer, courant, polar_mask, cutoff):
        build = by_kernel if fits else by_collectives
        parts = build(tracer, courant, polar_mask, cutoff, devices, bands)
        return advect(*parts, courant, bands)

    if not (fits and devices == 8 and clon % 144 == 0):
        return by_circles(tracer, courant, polar_mask, cutoff)
    half = clon * devices // 2
    _, _, padded = kept(cutoff, half)
    padded = jnp.where(polar_mask > 0, padded, 0).reshape(bands, clat)[:, ROWS_AT_EDGE:clat - ROWS_AT_EDGE]
    chunks = -(-jnp.max(padded.sum(axis=1)) // half) + 2 * ROWS_AT_EDGE
    return lax.cond(
        chunks <= LIMITS[-1],
        lambda *args: by_spectrum(*args, chunks, devices, bands),
        by_circles,
        tracer, courant, polar_mask, cutoff)


def solution(mesh):
    return jax.shard_map(
        on_device,
        mesh=mesh,
        in_specs=(P("lon", "lat", None), P(None, "lon", "lat", None), P(), P()),
        out_specs=P("lon", "lat", None),
        check_vma=False,
    )
```

```python
import functools
import math

import jax
import jax.numpy as jnp
import ml_dtypes
import numpy as np
from jax import lax
from jax.experimental import pallas as pl
from jax.experimental.pallas import tpu as pltpu
from jax.sharding import PartitionSpec as P

MESH = pl.DeviceIdType.MESH


def halves(table):
    high = table.astype(ml_dtypes.bfloat16)
    low = (table - high.astype(np.float64)).astype(ml_dtypes.bfloat16)
    return high, low


def hartley_tables(nlon):
    half = nlon // 2
    u = np.arange(half, dtype=np.int64)
    even = (u[:, None] * u[None, :]) % half * (2.0 * math.pi / half)
    odd = ((2 * u[:, None] + 1) * (2 * u[None, :] + 1)) % (2 * nlon) * (math.pi / nlon)
    cas = lambda t: np.cos(t) + np.sin(t)
    return (*halves(cas(even)), *halves(cas(odd)))


def split(x):
    high = x.astype(jnp.bfloat16)
    return high, (x - high.astype(jnp.float32)).astype(jnp.bfloat16)


def times(high, low, x):
    x_high, x_low = split(x)
    dot = functools.partial(jnp.dot, preferred_element_type=jnp.float32)
    return dot(high[...], x_high) + (dot(low[...], x_high) + dot(high[...], x_low))


def filter_kernel(devices, bands, chunks, mask_ref, cut_ref, tracer, courant, *rest):
    tables, rest = rest[:4], rest[4:]
    (out, before, after, edge_x, edge_y, ring, even_h, even_l, odd_h, odd_l,
     table_sem, send_a, recv_a, self_a, send_b, recv_b, self_b, send_e, recv_e) = rest
    me, lat = lax.axis_index("lon"), lax.axis_index("lat")
    clon, clat, nf = tracer.shape
    size = clat // devices // chunks
    nlon = clon * devices
    half = nlon // 2
    order = sorted(range(1, devices), key=lambda off: -min(off, devices - off))
    peers = [lax.rem(me + off, devices) for off in order]
    west = lax.rem(me + devices - 1, devices)
    north, south = lax.rem(lat + bands - 1, bands), lax.rem(lat + 1, bands)

    loads = [
        pltpu.make_async_copy(table, place, table_sem.at[i])
        for i, (table, place) in enumerate(zip(tables, (even_h, even_l, odd_h, odd_l)))
    ]
    for copy in loads:
        copy.start()

    barrier = pltpu.get_barrier_semaphore()
    for peer in peers:
        pl.semaphore_signal(barrier, inc=1, device_id={"lon": peer}, device_id_type=MESH)
    for band in (north, south):
        pl.semaphore_signal(barrier, inc=1, device_id={"lat": band}, device_id_type=MESH)
    pl.semaphore_wait(barrier, devices + 1)

    def first(owner, c):
        flip = owner // (devices // 2)
        tile = owner * chunks + c + flip * (chunks - 1 - 2 * c)
        return pl.multiple_of(tile * size, size)

    def landing(c):
        return ring.at[c, pl.ds(2 + me * clon, clon)]

    def result(owner, c):
        return ring.at[c, pl.ds(owner * clon, clon + 4)]

    def home(c):
        return out.at[:, pl.ds(first(me, c), size), :]

    def source(owner, c):
        return tracer.at[:, pl.ds(first(owner, c), size), :]

    there, back = [], []
    for c in range(chunks):
        own = pltpu.make_async_copy(source(me, c), landing(c), self_a.at[c])
        sent = [
            pltpu.make_async_remote_copy(
                source(peer, c), landing(c), send_a.at[c, j], recv_a.at[c, j],
                device_id={"lon": peer}, device_id_type=MESH)
            for j, peer in enumerate(peers)
        ]
        own.start()
        for copy in sent:
            copy.start()
        there.append((own, sent))

    def edge(src, dst, k, device):
        return pltpu.make_async_remote_copy(
            src, dst, send_e.at[k], recv_e.at[k], device_id=device, device_id_type=MESH)

    def inner(ref, start):
        return ref.at[pl.ds(2, clon), pl.ds(start, 8), :]

    go_x = edge(courant.at[0, pl.ds(0, 1)], edge_x, 0, {"lon": west})
    go_y = edge(courant.at[1, :, pl.ds(0, 8), :], edge_y, 1, {"lat": north})
    go_north = edge(inner(out, 0), after, 2, {"lat": north})
    go_south = edge(inner(out, clat - 8), before, 3, {"lat": south})
    go_x.start()
    go_y.start()
    for copy in loads:
        copy.wait()

    lane = lax.broadcasted_iota(jnp.int32, (1, 2 * nf), 1)
    index = lax.broadcasted_iota(jnp.int32, (half, 2 * nf), 0)
    scale = 1.0 / nlon

    for c in range(chunks):
        own, sent = there[c]
        own.wait()
        for copy in sent:
            copy.wait_recv()
        flat = ring.at[c].reshape((nlon + 4) * size, nf)
        first_row = lat * clat + first(me, c)

        def pair(p, carry):
            def block(start, count, r):
                return (pl.ds(start * size + r, count, stride=size), slice(None))

            def load(start):
                return jnp.concatenate(
                    [flat[block(start, half, 2 * p + s)] for s in range(2)], axis=1)

            row = first_row + 2 * p
            cut = jnp.where(lane < nf, cut_ref[row], cut_ref[row + 1])
            mask = jnp.where(lane < nf, mask_ref[row], mask_ref[row + 1])
            low, high = load(2), load(2 + half)
            even = times(even_h, even_l, low + high)
            odd = times(odd_h, odd_l, low - high)
            wave = 2 * index
            even = jnp.where(jnp.minimum(wave, nlon - wave) < cut, even * scale, 0.0)
            odd = jnp.where(jnp.minimum(wave + 1, nlon - 1 - wave) < cut, odd * scale, 0.0)
            even = times(even_h, even_l, even)
            odd = times(odd_h, odd_l, odd)
            low = jnp.where(mask > 0, even + odd, low)
            high = jnp.where(mask > 0, even - odd, high)
            for s in range(2):
                r = 2 * p + s
                lo, hi = low[:, s * nf:(s + 1) * nf], high[:, s * nf:(s + 1) * nf]
                flat[block(2, half, r)] = lo
                flat[block(2 + half, half, r)] = hi
                for e in range(2):
                    flat[pl.ds((2 + nlon + e) * size + r, 1), :] = lo[e:e + 1]
                    flat[pl.ds(e * size + r, 1), :] = hi[half - 2 + e:half - 1 + e]
            return carry

        lax.fori_loop(0, size // 2, pair, 0)

        own = pltpu.make_async_copy(result(me, c), home(c), self_b.at[c])
        sent = [
            pltpu.make_async_remote_copy(
                result(peer, c), home(c), send_b.at[c, j], recv_b.at[c, j],
                device_id={"lon": peer}, device_id_type=MESH)
            for j, peer in enumerate(peers)
        ]
        own.start()
        for copy in sent:
            copy.start()
        back.append((own, sent))

    for own, sent in there:
        for copy in sent:
            copy.wait_send()
    go_x.wait()
    for c in range(chunks):
        own, sent = back[c]
        own.wait()
        for copy in sent:
            copy.wait()
        if c == 0:
            @pl.when(lat > 0)
            def _():
                go_north.start()

            @pl.when(lat < bands - 1)
            def _():
                go_south.start()
    go_y.wait()

    @pl.when(lat > 0)
    def _():
        go_north.wait_send()
        go_south.wait_recv()

    @pl.when(lat < bands - 1)
    def _():
        go_south.wait_send()
        go_north.wait_recv()


def by_kernel(tracer, courant, polar_mask, cutoff, devices, bands):
    clon, clat, nf = tracer.shape
    nlon = clon * devices
    half = nlon // 2
    chunks = clat // devices // 8
    tables = [jnp.asarray(t) for t in hartley_tables(nlon)]
    smem = pl.BlockSpec(memory_space=pltpu.SMEM)
    hbm = pl.BlockSpec(memory_space=pltpu.HBM)
    dma = pltpu.SemaphoreType.DMA
    pairs, alone = dma((chunks, devices - 1)), dma((chunks,))
    shape = lambda *dims: jax.ShapeDtypeStruct(dims, jnp.float32)
    edge = shape(clon, 8, nf)
    return pl.pallas_call(
        functools.partial(filter_kernel, devices, bands, chunks),
        out_shape=(shape(clon + 4, clat, nf), edge, edge, shape(1, clat, nf), edge),
        in_specs=[smem, smem] + [hbm] * 6,
        out_specs=(hbm,) * 5,
        scratch_shapes=[pltpu.VMEM((chunks, nlon + 4, 8, nf), jnp.float32)]
        + [pltpu.VMEM((half, half), jnp.bfloat16)] * 4
        + [dma((4,)), pairs, pairs, alone, pairs, pairs, alone, dma((4,)), dma((4,))],
        compiler_params=pltpu.CompilerParams(
            collective_id=0, has_side_effects=True, vmem_limit_bytes=65000 << 10),
        name="filter_exchange",
    )(polar_mask, cutoff, tracer, courant, *tables)


def limited(far_low, low, high, far_high):
    face = (7.0 / 12.0) * (low + high) - (1.0 / 12.0) * (far_low + far_high)
    return jnp.minimum(jnp.maximum(face, jnp.minimum(low, high)), jnp.maximum(low, high))


def flux_kernel(bands, field, speed_x, next_x, edge_x, speed_y, edge_y, before, after, out, tall, flux):
    count, clat = out.shape[0], out.shape[1]
    final = pl.program_id(0) == pl.num_programs(0) - 1
    lat = lax.axis_index("lat")
    top, bottom = lat > 0, lat < bands - 1

    def flux_x(i, speed):
        return speed * limited(field[i], field[i + 1], field[i + 2], field[i + 3])

    def column(c, low_flux, speed):
        high_flux = flux_x(c + 1, speed)
        value = field[c + 2]
        tall[8:8 + clat] = value
        tall[0:8] = jnp.where(top, before[c], 0.0)
        tall[8 + clat:16 + clat] = jnp.where(bottom, after[c], 0.0)
        flux[0:clat] = speed_y[c] * limited(
            tall[6:6 + clat], tall[7:7 + clat], value, tall[9:9 + clat])
        flux[clat:clat + 1] = jnp.where(bottom, edge_y[c, 0:1], 0.0) * limited(
            tall[6 + clat:7 + clat], tall[7 + clat:8 + clat],
            tall[8 + clat:9 + clat], tall[9 + clat:10 + clat])
        out[c] = value - (high_flux - low_flux) - (flux[1:clat + 1] - flux[0:clat])
        return high_flux

    carry = flux_x(0, speed_x[0])
    carry = lax.fori_loop(0, count - 1, lambda c, low: column(c, low, speed_x[c + 1]), carry)
    column(count - 1, carry, jnp.where(final, edge_x[0], next_x[0]))


def advect(field, before, after, edge_x, edge_y, courant, bands):
    _, clon, clat, nf = courant.shape
    block = math.gcd(clon, 16)
    squeezed = pl.Squeezed()
    return pl.pallas_call(
        functools.partial(flux_kernel, bands),
        grid=(clon // block,),
        out_shape=jax.ShapeDtypeStruct((clon, clat, nf), jnp.float32),
        in_specs=[
            pl.BlockSpec((pl.Element(block + 4), pl.Element(clat), pl.Element(nf)),
                         lambda i: (i * block, 0, 0)),
            pl.BlockSpec((squeezed, block, clat, nf), lambda i: (0, i, 0, 0)),
            pl.BlockSpec((squeezed, 1, clat, nf),
                         lambda i: (0, jnp.minimum((i + 1) * block, clon - 1), 0, 0)),
            pl.BlockSpec((1, clat, nf), lambda i: (0, 0, 0)),
            pl.BlockSpec((squeezed, block, clat, nf), lambda i: (1, i, 0, 0)),
            pl.BlockSpec((block, 8, nf), lambda i: (i, 0, 0)),
            pl.BlockSpec((block, 8, nf), lambda i: (i, 0, 0)),
            pl.BlockSpec((block, 8, nf), lambda i: (i, 0, 0)),
        ],
        out_specs=pl.BlockSpec((block, clat, nf), lambda i: (i, 0, 0)),
        scratch_shapes=[pltpu.VMEM((clat + 16, nf), jnp.float32),
                        pltpu.VMEM((clat + 8, nf), jnp.float32)],
        compiler_params=pltpu.CompilerParams(vmem_limit_bytes=65000 << 10),
        name="flux_step",
    )(field, courant, courant, edge_x, courant, edge_y, before, after)


def by_collectives(tracer, courant, polar_mask, cutoff, devices, bands):
    clon, clat, nf = tracer.shape
    nlon, half = clon * devices, clon * devices // 2
    circles = lax.all_to_all(tracer, "lon", split_axis=1, concat_axis=0, tiled=True)
    rows = clat // devices
    start = lax.axis_index("lat") * clat + lax.axis_index("lon") * rows
    mask = lax.dynamic_slice_in_dim(polar_mask, start, rows)[None, :, None]
    cut = lax.dynamic_slice_in_dim(cutoff, start, rows)[None, :, None]
    tables = [jnp.asarray(t).astype(jnp.float32) for t in hartley_tables(nlon)]
    apply = lambda h, l, x: jnp.einsum("uk,krc->urc", h + l, x, precision=lax.Precision.HIGHEST)
    low, high = circles[:half], circles[half:]
    wave = 2 * lax.broadcasted_iota(jnp.int32, (half, 1, 1), 0)
    even = apply(tables[0], tables[1], low + high) * (1.0 / nlon)
    odd = apply(tables[2], tables[3], low - high) * (1.0 / nlon)
    even = jnp.where(jnp.minimum(wave, nlon - wave) < cut, even, 0.0)
    odd = jnp.where(jnp.minimum(wave + 1, nlon - 1 - wave) < cut, odd, 0.0)
    even = apply(tables[0], tables[1], even)
    odd = apply(tables[2], tables[3], odd)
    smooth = jnp.concatenate([even + odd, even - odd], axis=0)
    done = jnp.where(mask > 0, smooth, circles)
    field = lax.all_to_all(done, "lon", split_axis=0, concat_axis=1, tiled=True)
    up = [(i, (i + 1) % devices) for i in range(devices)]
    down = [(j, i) for i, j in up]
    before = lax.ppermute(field[clon - 2:], "lon", up)
    after = lax.ppermute(field[:2], "lon", down)
    wide = jnp.concatenate([before, field, after], axis=0)
    south = [(i, i + 1) for i in range(bands - 1)]
    north = [(j, i) for i, j in south]
    edge_x = lax.ppermute(courant[0, :1], "lon", down)
    edge_y = lax.ppermute(courant[1, :, :8], "lat", north)
    before = lax.ppermute(field[:, clat - 8:], "lat", south)
    after = lax.ppermute(field[:, :8], "lat", north)
    return wide, before, after, edge_x, edge_y


ROWS_AT_EDGE = 2
SKEW = 2
LAG = 2
AHEAD = 6
TAIL = 3 * SKEW + LAG + 2
BLOCK = 128
UNROLL = 8
LIMITS = ((36, 36), (42, 40), (48, 34), (54, 28), (60, 22), (66, 16), (72, 16))


def basis(nlon):
    half = nlon // 2
    i, n = np.arange(half), np.arange(nlon)
    tables = []
    for wave, sine in (((i + 1) // 2, (i % 2 == 0) & (i > 0)), (half - (i + 1) // 2, (i % 2 == 0) & (i > 0))):
        angle = (wave[:, None] * n[None, :]) % nlon * (2.0 * math.pi / nlon)
        size = np.where((wave == 0) | (wave == half), 1.0, 2.0) / nlon
        tables.append(np.where(sine[:, None], np.sin(angle), np.cos(angle)) * np.sqrt(size)[:, None])
    return np.stack(tables)


def forward_tables(nlon, devices):
    half, clon = nlon // 2, nlon // devices
    blocks = -(-half // BLOCK)
    whole = np.zeros((2, blocks * BLOCK, nlon))
    whole[:, :half] = basis(nlon)
    whole = whole.reshape(2 * blocks, BLOCK, devices, clon).transpose(2, 0, 1, 3)
    high, low = halves(whole)
    return np.concatenate([high, low, high], axis=-1)


def inverse_tables(nlon, devices):
    half, clon = nlon // 2, nlon // devices
    blocks = -(-half // BLOCK)
    whole = np.zeros((2, blocks * BLOCK, nlon))
    whole[:, :half] = basis(nlon)
    place = (np.arange(devices)[:, None] * clon + np.arange(clon + 16)[None, :] - 8) % nlon
    whole = whole[:, :, place].reshape(2 * blocks, BLOCK, devices, clon + 16).transpose(2, 0, 3, 1)
    high, low = halves(whole)
    return np.concatenate([high, low, high], axis=-1)


def kept(cut, half):
    low = 2 * cut - 1 <= half
    count = jnp.where(low, 2 * cut - 1, 2 * half + 1 - 2 * cut)
    return low, count, (count + 7) // 8 * 8


def forward_kernel(mask_ref, cut_ref, start_ref, tracer, tables, packed, x, table, out, todo, x_sem, table_sem, out_sem):
    me, lat = lax.axis_index("lon"), lax.axis_index("lat")
    clon, clat, nf = tracer.shape
    half = clon * 4
    blocks = -(-half // BLOCK)
    load = pltpu.make_async_copy(tables.at[me], table, table_sem)
    load.start()

    def read(row):
        return pltpu.make_async_copy(tracer.at[:, row, :], x.at[row], x_sem.at[row])

    def put(m, row, place):
        low, count, padded = kept(cut_ref[lat * clat + row], half)
        polar = mask_ref[lat * clat + row] > 0

        @pl.when(polar)
        def _():
            read(row).start()
            for b in range(blocks):
                todo[0, m + b] = place + b * BLOCK
                todo[1, m + b] = row
                todo[2, m + b] = jnp.where(low, 0, blocks) + b
                todo[3, m + b] = 1 if b == 0 else 0

        return (m + jnp.where(polar, (padded + BLOCK - 1) // BLOCK, 0), jnp.where(polar, padded, 0))

    m = jnp.int32(0)
    for i in range(2 * ROWS_AT_EDGE):
        m, _ = put(m, i if i < ROWS_AT_EDGE else clat - 2 * ROWS_AT_EDGE + i, i * half)

    def listed(row, carry):
        m, place = carry
        m, more = put(m, row, place)
        return m, place + more

    m, place = lax.fori_loop(ROWS_AT_EDGE, clat - ROWS_AT_EDGE, listed, (m, start_ref[0]))
    for u in range(UNROLL):
        todo[0, m + u] = place
        todo[1, m + u] = 0
        todo[2, m + u] = 0
        todo[3, m + u] = 0

    def write(c):
        at = pl.ds(pl.multiple_of(c * half, 8), half)
        return pltpu.make_async_copy(out.at[at], packed.at[at], out_sem.at[c])

    load.wait()

    def body(k, done):
        items = [k * UNROLL + u for u in range(UNROLL)]
        for j in items:
            @pl.when(todo[3, j] > 0)
            def _(j=j):
                read(todo[1, j]).wait()
        sums = []
        for j in items:
            high, rest = split(x[todo[1, j]])
            stack = jnp.concatenate([high, high, rest], axis=0)
            sums.append(jnp.dot(table[todo[2, j]], stack, preferred_element_type=jnp.float32))
        for j, value in zip(items, sums):
            out[pl.ds(pl.multiple_of(todo[0, j], 8), BLOCK), :] = value
        full = (done + 1) * half <= todo[0, items[-1]]

        @pl.when(full)
        def _():
            write(done).start()

        return done + jnp.where(full, 1, 0)

    done = lax.fori_loop(0, (m + UNROLL - 1) // UNROLL, body, jnp.int32(0))
    total = (place + half - 1) // half

    @pl.loop(done, total)
    def _(c):
        write(c).start()

    @pl.loop(0, total)
    def _(c):
        write(c).wait()


def exchange_kernel(bands, start_ref, packed, tracer, courant, totals, lon_low, lon_high, lat_low, lat_high,
                    edge_x, edge_y, own, mate, first, second, own_b, extra, own_sem, mate_send, mate_recv,
                    first_send, first_recv, second_send, second_recv, home_sem, home_send, home_recv,
                    own_b_sem, mate_b_send, mate_b_recv, lend_send, lend_recv, back_send, back_recv,
                    pass_send, pass_recv, band_send, band_recv, edge_send, edge_recv):
    me, lat = lax.axis_index("lon"), lax.axis_index("lat")
    clon, clat, nf = tracer.shape
    n, chunk = own.shape[0], own.shape[1]
    lent = own_b.shape[0]
    half = 2 * chunk
    fixed = 2 * ROWS_AT_EDGE
    base = fixed * half
    devices = 8
    z, core = me // 2, me % 2
    other = me + 1 - 2 * core
    outer = (z == 0) | (z == 3)
    inner = jnp.logical_not(outer)
    lender = (lat == 0) | (lat == 3)
    helper = jnp.logical_not(lender)
    pal = lat + 1 - 2 * (lat % 2)
    inward = lax.rem(jnp.where(z < 2, me + 2, me + devices - 2), devices)
    outward = lax.rem(jnp.where(z < 2, me + devices - 2, me + 2), devices)
    east, west = lax.rem(me + 1, devices), lax.rem(me + devices - 1, devices)
    north, south = lax.rem(lat + bands - 1, bands), lax.rem(lat + 1, bands)

    barrier = pltpu.get_barrier_semaphore()
    for peer in (other, inward, outward, east, west):
        pl.semaphore_signal(barrier, inc=1, device_id={"lon": peer}, device_id_type=MESH)
    for band in (north, south):
        for peer in (me, other):
            pl.semaphore_signal(barrier, inc=1, device_id={"lat": band, "lon": peer}, device_id_type=MESH)
    pl.semaphore_wait(barrier, 9)

    def part(c, which):
        return pl.ds(pl.multiple_of((2 * c + which) * chunk, 8), chunk)

    def part_b(c, which):
        return pl.ds(pl.multiple_of(n * half + (2 * (c - fixed) + which) * chunk, 8), chunk)

    def remote(src, dst, send, recv, **device):
        return pltpu.make_async_remote_copy(src, dst, send, recv, device_id=device, device_id_type=MESH)

    def to_own(c):
        return pltpu.make_async_copy(packed.at[part(c, core)], own.at[c], own_sem.at[c])

    def to_mate(c):
        return remote(packed.at[part(c, 1 - core)], mate.at[c], mate_send.at[c], mate_recv.at[c], lon=other)

    def to_own_b(c):
        return pltpu.make_async_copy(packed.at[part_b(c, core)], own_b.at[c], own_b_sem.at[c])

    def to_mate_b(c):
        return remote(packed.at[part_b(c, 1 - core)], extra.at[c], mate_b_send.at[c], mate_b_recv.at[c], lon=other)

    def lend(c):
        return remote(own_b.at[c], extra.at[c], lend_send.at[c], lend_recv.at[c], lat=pal)

    def out_first(c):
        return remote(own.at[c], first.at[c], first_send.at[c], first_recv.at[c], lon=inward)

    def in_second(c):
        return remote(first.at[c], second.at[c], first_send.at[c], second_recv.at[c], lon=inward)

    def out_second(c):
        return remote(second.at[c], second.at[c], second_send.at[c], second_recv.at[c], lon=outward)

    def place_b(c):
        return totals.at[pl.ds(pl.multiple_of(base + n * half + (2 * (c - fixed) + core) * chunk, 8), chunk)]

    def home(src, c):
        place = totals.at[pl.ds(pl.multiple_of(base + (2 * c + core) * chunk, 8), chunk)]
        return (pltpu.make_async_copy(src.at[c], place, home_sem.at[c]),
                remote(src.at[c], place, home_send.at[c], home_recv.at[c], lon=other))

    def give_back(src, c):
        return remote(src.at[c], place_b(c), back_send.at[c], back_recv.at[c], lat=pal)

    def pass_on(c):
        return remote(place_b(c), place_b(c), pass_send.at[c], pass_recv.at[c], lon=other)

    def bands_of(src, c):
        up = c < ROWS_AT_EDGE
        row = c + ROWS_AT_EDGE * (1 if up else -1)
        place = totals.at[pl.ds(pl.multiple_of(row * half + core * chunk, 8), chunk)]
        return [
            remote(src.at[c], place, band_send.at[c, q], band_recv.at[c, core],
                   lat=north if up else south, lon=peer)
            for q, peer in enumerate((me, other))
        ]

    def emit(src, c):
        for copy in home(src, c):
            copy.start()

        @pl.when(helper & (c >= fixed) & (c < lent))
        def _():
            give_back(src, c).start()

        for k in range(fixed):
            @pl.when((c == k) & ((lat > 0) if k < ROWS_AT_EDGE else (lat < bands - 1)))
            def _(k=k):
                for copy in bands_of(src, k):
                    copy.start()

    def load(c):
        to_own(c).start()
        to_mate(c).start()

        @pl.when(lender & (c + fixed < lent))
        def _():
            to_own_b(c + fixed).start()
            to_mate_b(c + fixed).start()

    @pl.loop(0, AHEAD)
    def _(c):
        load(c)

    def edge(src, dst, k, **device):
        return remote(src, dst, edge_send.at[k], edge_recv.at[k], **device)

    around = [edge(courant.at[0, pl.ds(0, 1)], edge_x, 0, lon=west),
              edge(tracer.at[pl.ds(0, 2)], lon_high, 1, lon=west),
              edge(tracer.at[pl.ds(clon - 2, 2)], lon_low, 2, lon=east)]
    go_north = [edge(courant.at[1, :, 0, :], edge_y.at[0], 3, lat=north)]
    go_south = []
    for k in range(ROWS_AT_EDGE):
        go_north.append(edge(tracer.at[:, k, :], lat_high.at[k], 4 + k, lat=north))
        go_south.append(edge(tracer.at[:, clat - ROWS_AT_EDGE + k, :], lat_low.at[k], 4 + ROWS_AT_EDGE + k, lat=south))

    index = lax.broadcasted_iota(jnp.int32, (chunk, nf), 0)

    @pl.loop(0, n + TAIL)
    def _(i):
        @pl.when(i + AHEAD < n)
        def _():
            load(i + AHEAD)

        @pl.when(i == n // 2)
        def _():
            for copy in around:
                copy.start()

            @pl.when(lat > 0)
            def _():
                for copy in go_north:
                    copy.start()

            @pl.when(lat < bands - 1)
            def _():
                for copy in go_south:
                    copy.start()

        @pl.when(lender & (i + fixed < lent))
        def _():
            c = i + fixed
            to_own_b(c).wait()
            to_mate_b(c).wait_recv()
            own_b[c] = own_b[c] + extra[c]
            lend(c).start()

        now = i

        @pl.when(now < n)
        def _():
            to_own(now).wait()
            to_mate(now).wait_recv()
            own[now] = own[now] + mate[now]

            @pl.when(helper & (now >= fixed) & (now < lent))
            def _():
                lend(now).wait_recv()
                borrowed = index + (2 * now + core) * chunk < start_ref[0]
                own[now] = jnp.where(borrowed, extra[now], own[now])

            @pl.when(outer)
            def _():
                out_first(now).start()

        @pl.when(inner & (now >= SKEW) & (now < n + SKEW))
        def _():
            c = now - SKEW
            out_first(c).wait_recv()
            first[c] = first[c] + own[c]
            in_second(c).start()

        @pl.when(inner & (now >= 2 * SKEW) & (now < n + 2 * SKEW))
        def _():
            c = now - 2 * SKEW
            in_second(c).wait_recv()
            far, mine = second[c], own[c]
            own[c] = first[c] + far
            second[c] = far + mine
            out_second(c).start()
            emit(own, c)

        @pl.when(outer & (now >= 3 * SKEW) & (now < n + 3 * SKEW))
        def _():
            c = now - 3 * SKEW
            out_second(c).wait_recv()
            second[c] = second[c] + own[c]
            emit(second, c)

        @pl.when(lender & (i >= fixed + 3 * SKEW + LAG) & (i < lent + 3 * SKEW + LAG))
        def _():
            c = i - 3 * SKEW - LAG
            give_back(own, c).wait_recv()
            pass_on(c).start()

        @pl.when(i >= TAIL)
        def _():
            c = i - TAIL
            to_mate(c).wait_send()
            out_first(c).wait_send()

            @pl.when(inner)
            def _():
                out_second(c).wait_send()

            here, away = home(own, c)
            here.wait()
            away.wait()

            @pl.when(lender & (c >= fixed) & (c < lent))
            def _():
                to_mate_b(c).wait_send()
                lend(c).wait_send()
                pass_on(c).wait()

            @pl.when(helper & (c >= fixed) & (c < lent))
            def _():
                give_back(own, c).wait_send()

    for copy in around:
        copy.wait()

    @pl.when(lat > 0)
    def _():
        for copy in go_north:
            copy.wait_send()
        for copy in go_south:
            copy.wait_recv()

    @pl.when(lat < bands - 1)
    def _():
        for copy in go_south:
            copy.wait_send()
        for copy in go_north:
            copy.wait_recv()

    for k in range(fixed):
        up = k < ROWS_AT_EDGE

        @pl.when((lat > 0) if up else (lat < bands - 1))
        def _(k=k):
            for copy in bands_of(own, k):
                copy.wait_send()

        @pl.when((lat < bands - 1) if up else (lat > 0))
        def _(k=k):
            for which in range(2):
                remote(own.at[k], own.at[k], band_send.at[k, 0], band_recv.at[k, which],
                       lat=north, lon=me).wait_recv()


def finish_kernel(bands, mask_ref, cut_ref, start_ref, totals, tracer, lon_low, lon_high, lat_low, lat_high,
                  edge_x, edge_y, courant, tables, out, field, speed_x, speed_y, side, ring, table, flux,
                  todo, load_sem, row_sem, x_sem, y_sem, ring_sem, out_sem):
    me, lat = lax.axis_index("lon"), lax.axis_index("lat")
    clon, clat, nf = tracer.shape
    half = clon * 4
    blocks = -(-half // BLOCK)
    deep = ring.shape[0]
    wide = clon + 16
    top, bottom = lat > 0, lat < bands - 1
    lead = ROWS_AT_EDGE
    mid = pl.ds(8, clon)

    loads = [
        pltpu.make_async_copy(src, dst, load_sem.at[k])
        for k, (src, dst) in enumerate((
            (tables.at[me], table),
            (lon_low, side.at[pl.ds(0, 2)]),
            (lon_high, side.at[pl.ds(2, 2)]),
            (edge_x, side.at[pl.ds(4, 1)]),
            (lat_low.at[0], field.at[0, mid]),
            (lat_low.at[1], field.at[1, mid]),
            (lat_high.at[0], field.at[clat + 2, mid]),
            (lat_high.at[1], field.at[clat + 3, mid]),
            (edge_y.at[0], speed_y.at[clat]),
        ))
    ]
    for copy in loads:
        copy.start()

    def cells(row):
        return pltpu.make_async_copy(tracer.at[:, row, :], field.at[row + lead, mid], row_sem.at[row])

    def along(row):
        return pltpu.make_async_copy(courant.at[0, :, row, :], speed_x.at[row, pl.ds(0, clon)], x_sem.at[row])

    def across(row):
        return pltpu.make_async_copy(courant.at[1, :, row, :], speed_y.at[row], y_sem.at[row])

    def result(row):
        return pltpu.make_async_copy(field.at[row, mid], out.at[:, row, :], out_sem.at[row])

    @pl.loop(0, clat)
    def _(row):
        cells(row).start()

    def put(m, entry, place):
        row = lat * clat + entry - lead
        valid = (row >= 0) & (row < bands * clat)
        row = jnp.clip(row, 0, bands * clat - 1)
        low, count, padded = kept(cut_ref[row], half)
        polar = valid & (mask_ref[row] > 0)

        @pl.when(polar)
        def _():
            for b in range(blocks):
                todo[0, m + b] = place + b * BLOCK
                todo[1, m + b] = entry
                todo[2, m + b] = jnp.where(low, 0, blocks) + b
                todo[3, m + b] = count - b * BLOCK

        return (m + jnp.where(polar, (padded + BLOCK - 1) // BLOCK, 0), jnp.where(polar, padded, 0))

    m = jnp.int32(0)
    base = 2 * lead * half
    for k in range(2 * lead):
        m, _ = put(m, k if k < lead else clat + k, k * half)
    for k in range(2 * lead):
        m, _ = put(m, lead + k if k < lead else clat - lead + k, base + k * half)

    def listed(entry, carry):
        m, place = carry
        m, more = put(m, entry, place)
        return m, place + more

    m, _ = lax.fori_loop(2 * lead, clat, listed, (m, base + start_ref[0]))
    for u in range(UNROLL):
        todo[0, m + u] = 0
        todo[1, m + u] = clat + 2 * lead
        todo[2, m + u] = blocks
        todo[3, m + u] = 0
    rounds = (m + UNROLL - 1) // UNROLL

    def fetch(j):
        slot = lax.rem(j, deep)
        return pltpu.make_async_copy(
            totals.at[pl.ds(pl.multiple_of(todo[0, j], 8), BLOCK)], ring.at[slot], ring_sem.at[slot])

    ahead = deep // UNROLL - 1
    for k in range(ahead):
        @pl.when(k < rounds)
        def _(k=k):
            for u in range(UNROLL):
                fetch(k * UNROLL + u).start()

    @pl.loop(0, clat)
    def _(row):
        across(row).start()
        along(row).start()

    for copy in loads:
        copy.wait()

    @pl.loop(0, clat)
    def _(row):
        cells(row).wait()

    zero = jnp.zeros((clon, nf), jnp.float32)

    @pl.when(jnp.logical_not(top))
    def _():
        field[0, 8:8 + clon] = zero
        field[1, 8:8 + clon] = zero

    @pl.when(jnp.logical_not(bottom))
    def _():
        field[clat + 2, 8:8 + clon] = zero
        field[clat + 3, 8:8 + clon] = zero
        speed_y[clat] = zero

    flat = field.reshape((clat + 2 * lead + 1) * wide, nf)
    for k, lon in enumerate((6, 7, clon + 8, clon + 9)):
        flat[pl.ds(lead * wide + lon, clat, stride=wide), :] = side[k]
    index = lax.broadcasted_iota(jnp.int32, (BLOCK, nf), 0)

    @pl.loop(0, rounds)
    def _(k):
        @pl.when(k + ahead < rounds)
        def _():
            for u in range(UNROLL):
                fetch((k + ahead) * UNROLL + u).start()

        items = [k * UNROLL + u for u in range(UNROLL)]
        for j in items:
            fetch(j).wait()
        parts = []
        for j in items:
            s = jnp.where(index < todo[3, j], ring[lax.rem(j, deep)], 0.0)
            s = jnp.where(todo[2, j] < blocks, s, -s)
            high, rest = split(s)
            parts.append(jnp.dot(table[todo[2, j]], jnp.concatenate([high, high, rest], axis=0),
                                 preferred_element_type=jnp.float32))
        for j, value in zip(items, parts):
            row = todo[1, j]
            field[row] = jnp.where(todo[2, j] == 0, value, field[row] + value)

    @pl.loop(0, clat)
    def _(row):
        across(row).wait()
        along(row).wait()

    flat_x = speed_x.reshape(clat * (clon + 8), nf)
    flat_x[pl.ds(clon, clat, stride=clon + 8), :] = side[4]

    def flux_y(i):
        f = lambda k: field[i + k, 8:8 + clon, :]
        return speed_y[i] * limited(f(0), f(1), f(2), f(3))

    def row_step(r, low_flux):
        high_flux = flux_y(r + 1)
        f = lambda start, count: field[r + lead, start:start + count, :]
        value = f(8, clon)
        flux[0:clon] = speed_x[r, 0:clon] * limited(f(6, clon), f(7, clon), value, f(9, clon))
        flux[clon:clon + 1] = speed_x[r, clon:clon + 1] * limited(
            f(6 + clon, 1), f(7 + clon, 1), f(8 + clon, 1), f(9 + clon, 1))
        field[r, 8:8 + clon, :] = value - (flux[1:clon + 1] - flux[0:clon]) - (high_flux - low_flux)
        result(r).start()
        return high_flux

    lax.fori_loop(0, clat, row_step, flux_y(0))

    @pl.loop(0, clat)
    def _(row):
        result(row).wait()


def by_spectrum(tracer, courant, polar_mask, cutoff, which, start, devices, bands):
    clon, clat, nf = tracer.shape
    nlon = clon * devices
    half = nlon // 2
    most = 2 * LIMITS[-1][0]
    items = (clat + 2 * ROWS_AT_EDGE) * -(-half // BLOCK) + 2 * UNROLL
    smem = pl.BlockSpec(memory_space=pltpu.SMEM)
    hbm = pl.BlockSpec(memory_space=pltpu.HBM)
    dma = pltpu.SemaphoreType.DMA
    shape = lambda *dims: jax.ShapeDtypeStruct(dims, jnp.float32)
    big = pltpu.CompilerParams(vmem_limit_bytes=65000 << 10)
    forward, inverse = forward_tables(nlon, devices), inverse_tables(nlon, devices)

    packed = pl.pallas_call(
        forward_kernel,
        out_shape=shape((most + 1) * half, nf),
        in_specs=[smem] * 3 + [hbm] * 2,
        out_specs=hbm,
        scratch_shapes=[
            pltpu.VMEM((clat, clon, nf), jnp.float32), pltpu.VMEM(forward.shape[1:], jnp.bfloat16),
            pltpu.VMEM(((most + 1) * half, nf), jnp.float32),
            pltpu.SMEM((4, items), jnp.int32),
            dma((clat,)), dma, dma((most + 1,))],
        compiler_params=big,
        name="forward",
    )(polar_mask, cutoff, start, tracer, jnp.asarray(forward))

    def exchange(n, lent, which):
        chunk = half // 2
        buffer, less = [pltpu.VMEM((k, chunk, nf), jnp.float32) for k in (n, lent)]

        def call(start, packed, tracer, courant):
            return pl.pallas_call(
                functools.partial(exchange_kernel, bands),
                out_shape=(shape((most + 2 * 2 * ROWS_AT_EDGE) * half, nf), shape(2, clat, nf), shape(2, clat, nf),
                           shape(2, clon, nf), shape(2, clon, nf), shape(1, clat, nf), shape(1, clon, nf)),
                in_specs=[smem] + [hbm] * 3,
                out_specs=(hbm,) * 7,
                scratch_shapes=[buffer] * 4 + [less] * 2 + [dma((n,))] * 10 + [dma((lent,))] * 9
                + [dma((2 * ROWS_AT_EDGE, 2)), dma((2 * ROWS_AT_EDGE, 2)), dma((8,)), dma((8,))],
                compiler_params=pltpu.CompilerParams(
                    collective_id=1 + which, has_side_effects=True, vmem_limit_bytes=65000 << 10),
                name=f"exchange_{n}",
            )(start, packed, tracer, courant)

        return call

    parts = lax.switch(which, [exchange(n, lent, i) for i, (n, lent) in enumerate(LIMITS)], start, packed, tracer, courant)

    return pl.pallas_call(
        functools.partial(finish_kernel, bands),
        out_shape=shape(clon, clat, nf),
        in_specs=[smem] * 3 + [hbm] * 10,
        out_specs=hbm,
        scratch_shapes=[
            pltpu.VMEM((clat + 2 * ROWS_AT_EDGE + 1, clon + 16, nf), jnp.float32),
            pltpu.VMEM((clat, clon + 8, nf), jnp.float32), pltpu.VMEM((clat + 1, clon, nf), jnp.float32),
            pltpu.VMEM((5, clat, nf), jnp.float32),
            pltpu.VMEM((4 * UNROLL, BLOCK, nf), jnp.float32), pltpu.VMEM(inverse.shape[1:], jnp.bfloat16),
            pltpu.VMEM((clon + 8, nf), jnp.float32),
            pltpu.SMEM((4, items), jnp.int32),
            dma((9,)), dma((clat,)), dma((clat,)), dma((clat,)), dma((4 * UNROLL,)), dma((clat,))],
        compiler_params=big,
        name="finish",
    )(polar_mask, cutoff, start, parts[0], tracer, *parts[1:], courant, jnp.asarray(inverse))


def on_device(tracer, courant, polar_mask, cutoff):
    devices, bands = lax.axis_size("lon"), lax.axis_size("lat")
    clon, clat, _ = tracer.shape
    fits = clat % (8 * devices) == 0 and bands > 2

    def by_circles(tracer, courant, polar_mask, cutoff):
        build = by_kernel if fits else by_collectives
        parts = build(tracer, courant, polar_mask, cutoff, devices, bands)
        return advect(*parts, courant, bands)

    if not (fits and devices == 8 and bands == 4 and clon % 144 == 0):
        return by_circles(tracer, courant, polar_mask, cutoff)
    half = clon * devices // 2
    fixed = 2 * ROWS_AT_EDGE
    _, _, padded = kept(cutoff, half)
    padded = jnp.where(polar_mask > 0, padded, 0).reshape(bands, clat)[:, ROWS_AT_EDGE:clat - ROWS_AT_EDGE]
    sums = padded.sum(axis=1)
    lent = jnp.stack([sums[0], sums[3]])
    light = jnp.stack([sums[1], sums[2]])
    need = (jnp.max(jnp.maximum((lent + light + 1) // 2, light)) + half - 1) // half + fixed
    whole = (jnp.max(lent) + half - 1) // half + 2 * fixed
    which = len(LIMITS)
    size = 0
    for i, (n, more) in reversed(list(enumerate(LIMITS))):
        enough = (need <= n) & (whole <= n + more)
        which = jnp.where(enough, i, which)
        size = jnp.where(enough, n, size)
    lat = lax.axis_index("lat")
    helper = (lat == 1) | (lat == 2)
    start = jnp.where(helper, size * half - jnp.where(lat == 1, sums[1], sums[2]), fixed * half)
    return lax.cond(
        which < len(LIMITS),
        lambda *args: by_spectrum(*args, which, start.reshape(1), devices, bands),
        by_circles,
        tracer, courant, polar_mask, cutoff)


def solution(mesh):
    return jax.shard_map(
        on_device,
        mesh=mesh,
        in_specs=(P("lon", "lat", None), P(None, "lon", "lat", None), P(), P()),
        out_specs=P("lon", "lat", None),
        check_vma=False,
    )
```

```python
import functools
import math

import jax
import jax.numpy as jnp
import ml_dtypes
import numpy as np
from jax import lax
from jax.experimental import pallas as pl
from jax.experimental.pallas import tpu as pltpu
from jax.sharding import PartitionSpec as P

MESH = pl.DeviceIdType.MESH


def halves(table):
    high = table.astype(ml_dtypes.bfloat16)
    low = (table - high.astype(np.float64)).astype(ml_dtypes.bfloat16)
    return high, low


def hartley_tables(nlon):
    half = nlon // 2
    u = np.arange(half, dtype=np.int64)
    even = (u[:, None] * u[None, :]) % half * (2.0 * math.pi / half)
    odd = ((2 * u[:, None] + 1) * (2 * u[None, :] + 1)) % (2 * nlon) * (math.pi / nlon)
    cas = lambda t: np.cos(t) + np.sin(t)
    return (*halves(cas(even)), *halves(cas(odd)))


def split(x):
    high = x.astype(jnp.bfloat16)
    return high, (x - high.astype(jnp.float32)).astype(jnp.bfloat16)


def times(high, low, x):
    x_high, x_low = split(x)
    dot = functools.partial(jnp.dot, preferred_element_type=jnp.float32)
    return dot(high[...], x_high) + (dot(low[...], x_high) + dot(high[...], x_low))


def filter_kernel(devices, bands, chunks, mask_ref, cut_ref, tracer, courant, *rest):
    tables, rest = rest[:4], rest[4:]
    (out, before, after, edge_x, edge_y, ring, even_h, even_l, odd_h, odd_l,
     table_sem, send_a, recv_a, self_a, send_b, recv_b, self_b, send_e, recv_e) = rest
    me, lat = lax.axis_index("lon"), lax.axis_index("lat")
    clon, clat, nf = tracer.shape
    size = clat // devices // chunks
    nlon = clon * devices
    half = nlon // 2
    order = sorted(range(1, devices), key=lambda off: -min(off, devices - off))
    peers = [lax.rem(me + off, devices) for off in order]
    west = lax.rem(me + devices - 1, devices)
    north, south = lax.rem(lat + bands - 1, bands), lax.rem(lat + 1, bands)

    loads = [
        pltpu.make_async_copy(table, place, table_sem.at[i])
        for i, (table, place) in enumerate(zip(tables, (even_h, even_l, odd_h, odd_l)))
    ]
    for copy in loads:
        copy.start()

    barrier = pltpu.get_barrier_semaphore()
    for peer in peers:
        pl.semaphore_signal(barrier, inc=1, device_id={"lon": peer}, device_id_type=MESH)
    for band in (north, south):
        pl.semaphore_signal(barrier, inc=1, device_id={"lat": band}, device_id_type=MESH)
    pl.semaphore_wait(barrier, devices + 1)

    def first(owner, c):
        flip = owner // (devices // 2)
        tile = owner * chunks + c + flip * (chunks - 1 - 2 * c)
        return pl.multiple_of(tile * size, size)

    def landing(c):
        return ring.at[c, pl.ds(2 + me * clon, clon)]

    def result(owner, c):
        return ring.at[c, pl.ds(owner * clon, clon + 4)]

    def home(c):
        return out.at[:, pl.ds(first(me, c), size), :]

    def source(owner, c):
        return tracer.at[:, pl.ds(first(owner, c), size), :]

    there, back = [], []
    for c in range(chunks):
        own = pltpu.make_async_copy(source(me, c), landing(c), self_a.at[c])
        sent = [
            pltpu.make_async_remote_copy(
                source(peer, c), landing(c), send_a.at[c, j], recv_a.at[c, j],
                device_id={"lon": peer}, device_id_type=MESH)
            for j, peer in enumerate(peers)
        ]
        own.start()
        for copy in sent:
            copy.start()
        there.append((own, sent))

    def edge(src, dst, k, device):
        return pltpu.make_async_remote_copy(
            src, dst, send_e.at[k], recv_e.at[k], device_id=device, device_id_type=MESH)

    def inner(ref, start):
        return ref.at[pl.ds(2, clon), pl.ds(start, 8), :]

    go_x = edge(courant.at[0, pl.ds(0, 1)], edge_x, 0, {"lon": west})
    go_y = edge(courant.at[1, :, pl.ds(0, 8), :], edge_y, 1, {"lat": north})
    go_north = edge(inner(out, 0), after, 2, {"lat": north})
    go_south = edge(inner(out, clat - 8), before, 3, {"lat": south})
    go_x.start()
    go_y.start()
    for copy in loads:
        copy.wait()

    lane = lax.broadcasted_iota(jnp.int32, (1, 2 * nf), 1)
    index = lax.broadcasted_iota(jnp.int32, (half, 2 * nf), 0)
    scale = 1.0 / nlon

    for c in range(chunks):
        own, sent = there[c]
        own.wait()
        for copy in sent:
            copy.wait_recv()
        flat = ring.at[c].reshape((nlon + 4) * size, nf)
        first_row = lat * clat + first(me, c)

        def pair(p, carry):
            def block(start, count, r):
                return (pl.ds(start * size + r, count, stride=size), slice(None))

            def load(start):
                return jnp.concatenate(
                    [flat[block(start, half, 2 * p + s)] for s in range(2)], axis=1)

            row = first_row + 2 * p
            cut = jnp.where(lane < nf, cut_ref[row], cut_ref[row + 1])
            mask = jnp.where(lane < nf, mask_ref[row], mask_ref[row + 1])
            low, high = load(2), load(2 + half)
            even = times(even_h, even_l, low + high)
            odd = times(odd_h, odd_l, low - high)
            wave = 2 * index
            even = jnp.where(jnp.minimum(wave, nlon - wave) < cut, even * scale, 0.0)
            odd = jnp.where(jnp.minimum(wave + 1, nlon - 1 - wave) < cut, odd * scale, 0.0)
            even = times(even_h, even_l, even)
            odd = times(odd_h, odd_l, odd)
            low = jnp.where(mask > 0, even + odd, low)
            high = jnp.where(mask > 0, even - odd, high)
            for s in range(2):
                r = 2 * p + s
                lo, hi = low[:, s * nf:(s + 1) * nf], high[:, s * nf:(s + 1) * nf]
                flat[block(2, half, r)] = lo
                flat[block(2 + half, half, r)] = hi
                for e in range(2):
                    flat[pl.ds((2 + nlon + e) * size + r, 1), :] = lo[e:e + 1]
                    flat[pl.ds(e * size + r, 1), :] = hi[half - 2 + e:half - 1 + e]
            return carry

        lax.fori_loop(0, size // 2, pair, 0)

        own = pltpu.make_async_copy(result(me, c), home(c), self_b.at[c])
        sent = [
            pltpu.make_async_remote_copy(
                result(peer, c), home(c), send_b.at[c, j], recv_b.at[c, j],
                device_id={"lon": peer}, device_id_type=MESH)
            for j, peer in enumerate(peers)
        ]
        own.start()
        for copy in sent:
            copy.start()
        back.append((own, sent))

    for own, sent in there:
        for copy in sent:
            copy.wait_send()
    go_x.wait()
    for c in range(chunks):
        own, sent = back[c]
        own.wait()
        for copy in sent:
            copy.wait()
        if c == 0:
            @pl.when(lat > 0)
            def _():
                go_north.start()

            @pl.when(lat < bands - 1)
            def _():
                go_south.start()
    go_y.wait()

    @pl.when(lat > 0)
    def _():
        go_north.wait_send()
        go_south.wait_recv()

    @pl.when(lat < bands - 1)
    def _():
        go_south.wait_send()
        go_north.wait_recv()


def by_kernel(tracer, courant, polar_mask, cutoff, devices, bands):
    clon, clat, nf = tracer.shape
    nlon = clon * devices
    half = nlon // 2
    chunks = clat // devices // 8
    tables = [jnp.asarray(t) for t in hartley_tables(nlon)]
    smem = pl.BlockSpec(memory_space=pltpu.SMEM)
    hbm = pl.BlockSpec(memory_space=pltpu.HBM)
    dma = pltpu.SemaphoreType.DMA
    pairs, alone = dma((chunks, devices - 1)), dma((chunks,))
    shape = lambda *dims: jax.ShapeDtypeStruct(dims, jnp.float32)
    edge = shape(clon, 8, nf)
    return pl.pallas_call(
        functools.partial(filter_kernel, devices, bands, chunks),
        out_shape=(shape(clon + 4, clat, nf), edge, edge, shape(1, clat, nf), edge),
        in_specs=[smem, smem] + [hbm] * 6,
        out_specs=(hbm,) * 5,
        scratch_shapes=[pltpu.VMEM((chunks, nlon + 4, 8, nf), jnp.float32)]
        + [pltpu.VMEM((half, half), jnp.bfloat16)] * 4
        + [dma((4,)), pairs, pairs, alone, pairs, pairs, alone, dma((4,)), dma((4,))],
        compiler_params=pltpu.CompilerParams(
            collective_id=0, has_side_effects=True, vmem_limit_bytes=65000 << 10),
        name="filter_exchange",
    )(polar_mask, cutoff, tracer, courant, *tables)


def limited(far_low, low, high, far_high):
    face = (7.0 / 12.0) * (low + high) - (1.0 / 12.0) * (far_low + far_high)
    return jnp.minimum(jnp.maximum(face, jnp.minimum(low, high)), jnp.maximum(low, high))


def flux_kernel(bands, field, speed_x, next_x, edge_x, speed_y, edge_y, before, after, out, tall, flux):
    count, clat = out.shape[0], out.shape[1]
    final = pl.program_id(0) == pl.num_programs(0) - 1
    lat = lax.axis_index("lat")
    top, bottom = lat > 0, lat < bands - 1

    def flux_x(i, speed):
        return speed * limited(field[i], field[i + 1], field[i + 2], field[i + 3])

    def column(c, low_flux, speed):
        high_flux = flux_x(c + 1, speed)
        value = field[c + 2]
        tall[8:8 + clat] = value
        tall[0:8] = jnp.where(top, before[c], 0.0)
        tall[8 + clat:16 + clat] = jnp.where(bottom, after[c], 0.0)
        flux[0:clat] = speed_y[c] * limited(
            tall[6:6 + clat], tall[7:7 + clat], value, tall[9:9 + clat])
        flux[clat:clat + 1] = jnp.where(bottom, edge_y[c, 0:1], 0.0) * limited(
            tall[6 + clat:7 + clat], tall[7 + clat:8 + clat],
            tall[8 + clat:9 + clat], tall[9 + clat:10 + clat])
        out[c] = value - (high_flux - low_flux) - (flux[1:clat + 1] - flux[0:clat])
        return high_flux

    carry = flux_x(0, speed_x[0])
    carry = lax.fori_loop(0, count - 1, lambda c, low: column(c, low, speed_x[c + 1]), carry)
    column(count - 1, carry, jnp.where(final, edge_x[0], next_x[0]))


def advect(field, before, after, edge_x, edge_y, courant, bands):
    _, clon, clat, nf = courant.shape
    block = math.gcd(clon, 16)
    squeezed = pl.Squeezed()
    return pl.pallas_call(
        functools.partial(flux_kernel, bands),
        grid=(clon // block,),
        out_shape=jax.ShapeDtypeStruct((clon, clat, nf), jnp.float32),
        in_specs=[
            pl.BlockSpec((pl.Element(block + 4), pl.Element(clat), pl.Element(nf)),
                         lambda i: (i * block, 0, 0)),
            pl.BlockSpec((squeezed, block, clat, nf), lambda i: (0, i, 0, 0)),
            pl.BlockSpec((squeezed, 1, clat, nf),
                         lambda i: (0, jnp.minimum((i + 1) * block, clon - 1), 0, 0)),
            pl.BlockSpec((1, clat, nf), lambda i: (0, 0, 0)),
            pl.BlockSpec((squeezed, block, clat, nf), lambda i: (1, i, 0, 0)),
            pl.BlockSpec((block, 8, nf), lambda i: (i, 0, 0)),
            pl.BlockSpec((block, 8, nf), lambda i: (i, 0, 0)),
            pl.BlockSpec((block, 8, nf), lambda i: (i, 0, 0)),
        ],
        out_specs=pl.BlockSpec((block, clat, nf), lambda i: (i, 0, 0)),
        scratch_shapes=[pltpu.VMEM((clat + 16, nf), jnp.float32),
                        pltpu.VMEM((clat + 8, nf), jnp.float32)],
        compiler_params=pltpu.CompilerParams(vmem_limit_bytes=65000 << 10),
        name="flux_step",
    )(field, courant, courant, edge_x, courant, edge_y, before, after)


def by_collectives(tracer, courant, polar_mask, cutoff, devices, bands):
    clon, clat, nf = tracer.shape
    nlon, half = clon * devices, clon * devices // 2
    circles = lax.all_to_all(tracer, "lon", split_axis=1, concat_axis=0, tiled=True)
    rows = clat // devices
    start = lax.axis_index("lat") * clat + lax.axis_index("lon") * rows
    mask = lax.dynamic_slice_in_dim(polar_mask, start, rows)[None, :, None]
    cut = lax.dynamic_slice_in_dim(cutoff, start, rows)[None, :, None]
    tables = [jnp.asarray(t).astype(jnp.float32) for t in hartley_tables(nlon)]
    apply = lambda h, l, x: jnp.einsum("uk,krc->urc", h + l, x, precision=lax.Precision.HIGHEST)
    low, high = circles[:half], circles[half:]
    wave = 2 * lax.broadcasted_iota(jnp.int32, (half, 1, 1), 0)
    even = apply(tables[0], tables[1], low + high) * (1.0 / nlon)
    odd = apply(tables[2], tables[3], low - high) * (1.0 / nlon)
    even = jnp.where(jnp.minimum(wave, nlon - wave) < cut, even, 0.0)
    odd = jnp.where(jnp.minimum(wave + 1, nlon - 1 - wave) < cut, odd, 0.0)
    even = apply(tables[0], tables[1], even)
    odd = apply(tables[2], tables[3], odd)
    smooth = jnp.concatenate([even + odd, even - odd], axis=0)
    done = jnp.where(mask > 0, smooth, circles)
    field = lax.all_to_all(done, "lon", split_axis=0, concat_axis=1, tiled=True)
    up = [(i, (i + 1) % devices) for i in range(devices)]
    down = [(j, i) for i, j in up]
    before = lax.ppermute(field[clon - 2:], "lon", up)
    after = lax.ppermute(field[:2], "lon", down)
    wide = jnp.concatenate([before, field, after], axis=0)
    south = [(i, i + 1) for i in range(bands - 1)]
    north = [(j, i) for i, j in south]
    edge_x = lax.ppermute(courant[0, :1], "lon", down)
    edge_y = lax.ppermute(courant[1, :, :8], "lat", north)
    before = lax.ppermute(field[:, clat - 8:], "lat", south)
    after = lax.ppermute(field[:, :8], "lat", north)
    return wide, before, after, edge_x, edge_y


ROWS_AT_EDGE = 2
SKEW = 2
LAG = 2
AHEAD = 6
TAIL = 3 * SKEW + LAG + 2
BLOCK = 128
UNROLL = 16
LIMITS = ((36, 36), (39, 39), (42, 40), (45, 37), (48, 34), (51, 31), (54, 28), (57, 25), (60, 22), (63, 19), (66, 16), (70, 16))


def basis(nlon):
    half = nlon // 2
    i, n = np.arange(half), np.arange(nlon)
    tables = []
    for wave, sine in (((i + 1) // 2, (i % 2 == 0) & (i > 0)), (half - (i + 1) // 2, (i % 2 == 0) & (i > 0))):
        angle = (wave[:, None] * n[None, :]) % nlon * (2.0 * math.pi / nlon)
        size = np.where((wave == 0) | (wave == half), 1.0, 2.0) / nlon
        tables.append(np.where(sine[:, None], np.sin(angle), np.cos(angle)) * np.sqrt(size)[:, None])
    return np.stack(tables)


def forward_tables(nlon, devices):
    half, clon = nlon // 2, nlon // devices
    blocks = -(-half // BLOCK)
    whole = np.zeros((2, blocks * BLOCK, nlon))
    whole[:, :half] = basis(nlon)
    whole = whole.reshape(2 * blocks, BLOCK, devices, clon).transpose(2, 0, 1, 3)
    high, low = halves(whole)
    return np.concatenate([high, low, high], axis=-1)


def inverse_tables(nlon, devices):
    half, clon = nlon // 2, nlon // devices
    blocks = -(-half // BLOCK)
    whole = np.zeros((2, blocks * BLOCK, nlon))
    whole[:, :half] = basis(nlon)
    place = (np.arange(devices)[:, None] * clon + np.arange(clon + 16)[None, :] - 8) % nlon
    whole = whole[:, :, place].reshape(2 * blocks, BLOCK, devices, clon + 16).transpose(2, 0, 3, 1)
    high, low = halves(whole)
    return np.concatenate([high, low, high], axis=-1)


def kept(cut, half):
    low = 2 * cut - 1 <= half
    count = jnp.where(low, 2 * cut - 1, 2 * half + 1 - 2 * cut)
    return low, count, (count + 7) // 8 * 8


def forward_kernel(mask_ref, cut_ref, start_ref, tracer, tables, packed, x, table, out, todo, x_sem, table_sem, out_sem):
    me, lat = lax.axis_index("lon"), lax.axis_index("lat")
    clon, clat, nf = tracer.shape
    half = clon * 4
    blocks = -(-half // BLOCK)
    load = pltpu.make_async_copy(tables.at[me], table, table_sem)
    load.start()

    def read(row):
        return pltpu.make_async_copy(tracer.at[:, row, :], x.at[row], x_sem.at[row])

    def put(m, row, place):
        low, count, padded = kept(cut_ref[lat * clat + row], half)
        polar = mask_ref[lat * clat + row] > 0

        @pl.when(polar)
        def _():
            read(row).start()
            for b in range(blocks):
                todo[0, m + b] = place + b * BLOCK
                todo[1, m + b] = row
                todo[2, m + b] = jnp.where(low, 0, blocks) + b
                todo[3, m + b] = 1 if b == 0 else 0

        return (m + jnp.where(polar, (padded + BLOCK - 1) // BLOCK, 0), jnp.where(polar, padded, 0))

    m = jnp.int32(0)
    for i in range(2 * ROWS_AT_EDGE):
        m, _ = put(m, i if i < ROWS_AT_EDGE else clat - 2 * ROWS_AT_EDGE + i, i * half)

    def listed(row, carry):
        m, place = carry
        m, more = put(m, row, place)
        return m, place + more

    m, place = lax.fori_loop(ROWS_AT_EDGE, clat - ROWS_AT_EDGE, listed, (m, start_ref[0]))
    for u in range(UNROLL):
        todo[0, m + u] = place
        todo[1, m + u] = 0
        todo[2, m + u] = 0
        todo[3, m + u] = 0

    def write(c):
        at = pl.ds(pl.multiple_of(c * half, 8), half)
        return pltpu.make_async_copy(out.at[at], packed.at[at], out_sem.at[c])

    load.wait()

    def body(k, done):
        items = [k * UNROLL + u for u in range(UNROLL)]
        for j in items:
            @pl.when(todo[3, j] > 0)
            def _(j=j):
                read(todo[1, j]).wait()
        sums = []
        for j in items:
            high, rest = split(x[todo[1, j]])
            stack = jnp.concatenate([high, high, rest], axis=0)
            sums.append(jnp.dot(table[todo[2, j]], stack, preferred_element_type=jnp.float32))
        for j, value in zip(items, sums):
            out[pl.ds(pl.multiple_of(todo[0, j], 8), BLOCK), :] = value
        full = (done + 1) * half <= todo[0, items[-1]]

        @pl.when(full)
        def _():
            write(done).start()

        return done + jnp.where(full, 1, 0)

    done = lax.fori_loop(0, (m + UNROLL - 1) // UNROLL, body, jnp.int32(0))
    total = (place + half - 1) // half

    @pl.loop(done, total)
    def _(c):
        write(c).start()

    @pl.loop(0, total)
    def _(c):
        write(c).wait()


def exchange_kernel(bands, start_ref, packed, tracer, courant, totals, lon_low, lon_high, lat_low, lat_high,
                    edge_x, edge_y, own, mate, first, second, own_b, extra, own_sem, mate_send, mate_recv,
                    first_send, first_recv, second_send, second_recv, home_sem, home_send, home_recv,
                    own_b_sem, mate_b_send, mate_b_recv, lend_send, lend_recv, back_send, back_recv,
                    pass_send, pass_recv, band_send, band_recv, edge_send, edge_recv):
    me, lat = lax.axis_index("lon"), lax.axis_index("lat")
    clon, clat, nf = tracer.shape
    n, chunk = own.shape[0], own.shape[1]
    lent = own_b.shape[0]
    half = 2 * chunk
    fixed = 2 * ROWS_AT_EDGE
    base = fixed * half
    devices = 8
    z, core = me // 2, me % 2
    other = me + 1 - 2 * core
    outer = (z == 0) | (z == 3)
    inner = jnp.logical_not(outer)
    lender = (lat == 0) | (lat == 3)
    helper = jnp.logical_not(lender)
    pal = lat + 1 - 2 * (lat % 2)
    inward = lax.rem(jnp.where(z < 2, me + 2, me + devices - 2), devices)
    outward = lax.rem(jnp.where(z < 2, me + devices - 2, me + 2), devices)
    east, west = lax.rem(me + 1, devices), lax.rem(me + devices - 1, devices)
    north, south = lax.rem(lat + bands - 1, bands), lax.rem(lat + 1, bands)

    barrier = pltpu.get_barrier_semaphore()
    for peer in (other, inward, outward, east, west):
        pl.semaphore_signal(barrier, inc=1, device_id={"lon": peer}, device_id_type=MESH)
    for band in (north, south):
        for peer in (me, other):
            pl.semaphore_signal(barrier, inc=1, device_id={"lat": band, "lon": peer}, device_id_type=MESH)
    pl.semaphore_wait(barrier, 9)

    def part(c, which):
        return pl.ds(pl.multiple_of((2 * c + which) * chunk, 8), chunk)

    def part_b(c, which):
        return pl.ds(pl.multiple_of(n * half + (2 * (c - fixed) + which) * chunk, 8), chunk)

    def remote(src, dst, send, recv, **device):
        return pltpu.make_async_remote_copy(src, dst, send, recv, device_id=device, device_id_type=MESH)

    def to_own(c):
        return pltpu.make_async_copy(packed.at[part(c, core)], own.at[c], own_sem.at[c])

    def to_mate(c):
        return remote(packed.at[part(c, 1 - core)], mate.at[c], mate_send.at[c], mate_recv.at[c], lon=other)

    def to_own_b(c):
        return pltpu.make_async_copy(packed.at[part_b(c, core)], own_b.at[c], own_b_sem.at[c])

    def to_mate_b(c):
        return remote(packed.at[part_b(c, 1 - core)], extra.at[c], mate_b_send.at[c], mate_b_recv.at[c], lon=other)

    def lend(c):
        return remote(own_b.at[c], extra.at[c], lend_send.at[c], lend_recv.at[c], lat=pal)

    def out_first(c):
        return remote(own.at[c], first.at[c], first_send.at[c], first_recv.at[c], lon=inward)

    def in_second(c):
        return remote(first.at[c], second.at[c], first_send.at[c], second_recv.at[c], lon=inward)

    def out_second(c):
        return remote(second.at[c], second.at[c], second_send.at[c], second_recv.at[c], lon=outward)

    def place_b(c):
        return totals.at[pl.ds(pl.multiple_of(base + n * half + (2 * (c - fixed) + core) * chunk, 8), chunk)]

    def home(src, c):
        place = totals.at[pl.ds(pl.multiple_of(base + (2 * c + core) * chunk, 8), chunk)]
        return (pltpu.make_async_copy(src.at[c], place, home_sem.at[c]),
                remote(src.at[c], place, home_send.at[c], home_recv.at[c], lon=other))

    def give_back(src, c):
        return remote(src.at[c], place_b(c), back_send.at[c], back_recv.at[c], lat=pal)

    def pass_on(c):
        return remote(place_b(c), place_b(c), pass_send.at[c], pass_recv.at[c], lon=other)

    def bands_of(src, c):
        up = c < ROWS_AT_EDGE
        row = c + ROWS_AT_EDGE * (1 if up else -1)
        place = totals.at[pl.ds(pl.multiple_of(row * half + core * chunk, 8), chunk)]
        return [
            remote(src.at[c], place, band_send.at[c, q], band_recv.at[c, core],
                   lat=north if up else south, lon=peer)
            for q, peer in enumerate((me, other))
        ]

    def emit(src, c):
        for copy in home(src, c):
            copy.start()

        @pl.when(helper & (c >= fixed) & (c < lent))
        def _():
            give_back(src, c).start()

        for k in range(fixed):
            @pl.when((c == k) & ((lat > 0) if k < ROWS_AT_EDGE else (lat < bands - 1)))
            def _(k=k):
                for copy in bands_of(src, k):
                    copy.start()

    def load(c):
        to_own(c).start()
        to_mate(c).start()

        @pl.when(lender & (c + fixed < lent))
        def _():
            to_own_b(c + fixed).start()
            to_mate_b(c + fixed).start()

    @pl.loop(0, AHEAD)
    def _(c):
        load(c)

    def edge(src, dst, k, **device):
        return remote(src, dst, edge_send.at[k], edge_recv.at[k], **device)

    around = [edge(courant.at[0, pl.ds(0, 1)], edge_x, 0, lon=west),
              edge(tracer.at[pl.ds(0, 2)], lon_high, 1, lon=west),
              edge(tracer.at[pl.ds(clon - 2, 2)], lon_low, 2, lon=east)]
    go_north = [edge(courant.at[1, :, 0, :], edge_y.at[0], 3, lat=north)]
    go_south = []
    for k in range(ROWS_AT_EDGE):
        go_north.append(edge(tracer.at[:, k, :], lat_high.at[k], 4 + k, lat=north))
        go_south.append(edge(tracer.at[:, clat - ROWS_AT_EDGE + k, :], lat_low.at[k], 4 + ROWS_AT_EDGE + k, lat=south))

    index = lax.broadcasted_iota(jnp.int32, (chunk, nf), 0)

    @pl.loop(0, n + TAIL)
    def _(i):
        @pl.when(i + AHEAD < n)
        def _():
            load(i + AHEAD)

        @pl.when(i == n // 2)
        def _():
            for copy in around:
                copy.start()

            @pl.when(lat > 0)
            def _():
                for copy in go_north:
                    copy.start()

            @pl.when(lat < bands - 1)
            def _():
                for copy in go_south:
                    copy.start()

        @pl.when(lender & (i + fixed < lent))
        def _():
            c = i + fixed
            to_own_b(c).wait()
            to_mate_b(c).wait_recv()
            own_b[c] = own_b[c] + extra[c]
            lend(c).start()

        now = i

        @pl.when(now < n)
        def _():
            to_own(now).wait()
            to_mate(now).wait_recv()
            own[now] = own[now] + mate[now]

            @pl.when(helper & (now >= fixed) & (now < lent))
            def _():
                lend(now).wait_recv()
                borrowed = index + (2 * now + core) * chunk < start_ref[0]
                own[now] = jnp.where(borrowed, extra[now], own[now])

            @pl.when(outer)
            def _():
                out_first(now).start()

        @pl.when(inner & (now >= SKEW) & (now < n + SKEW))
        def _():
            c = now - SKEW
            out_first(c).wait_recv()
            first[c] = first[c] + own[c]
            in_second(c).start()

        @pl.when(inner & (now >= 2 * SKEW) & (now < n + 2 * SKEW))
        def _():
            c = now - 2 * SKEW
            in_second(c).wait_recv()
            far, mine = second[c], own[c]
            own[c] = first[c] + far
            second[c] = far + mine
            out_second(c).start()
            emit(own, c)

        @pl.when(outer & (now >= 3 * SKEW) & (now < n + 3 * SKEW))
        def _():
            c = now - 3 * SKEW
            out_second(c).wait_recv()
            second[c] = second[c] + own[c]
            emit(second, c)

        @pl.when(lender & (i >= fixed + 3 * SKEW + LAG) & (i < lent + 3 * SKEW + LAG))
        def _():
            c = i - 3 * SKEW - LAG
            give_back(own, c).wait_recv()
            pass_on(c).start()

        @pl.when(i >= TAIL)
        def _():
            c = i - TAIL
            to_mate(c).wait_send()
            out_first(c).wait_send()

            @pl.when(inner)
            def _():
                out_second(c).wait_send()

            here, away = home(own, c)
            here.wait()
            away.wait()

            @pl.when(lender & (c >= fixed) & (c < lent))
            def _():
                to_mate_b(c).wait_send()
                lend(c).wait_send()
                pass_on(c).wait()

            @pl.when(helper & (c >= fixed) & (c < lent))
            def _():
                give_back(own, c).wait_send()

    for copy in around:
        copy.wait()

    @pl.when(lat > 0)
    def _():
        for copy in go_north:
            copy.wait_send()
        for copy in go_south:
            copy.wait_recv()

    @pl.when(lat < bands - 1)
    def _():
        for copy in go_south:
            copy.wait_send()
        for copy in go_north:
            copy.wait_recv()

    for k in range(fixed):
        up = k < ROWS_AT_EDGE

        @pl.when((lat > 0) if up else (lat < bands - 1))
        def _(k=k):
            for copy in bands_of(own, k):
                copy.wait_send()

        @pl.when((lat < bands - 1) if up else (lat > 0))
        def _(k=k):
            for which in range(2):
                remote(own.at[k], own.at[k], band_send.at[k, 0], band_recv.at[k, which],
                       lat=north, lon=me).wait_recv()


def finish_kernel(bands, mask_ref, cut_ref, start_ref, totals, tracer, lon_low, lon_high, lat_low, lat_high,
                  edge_x, edge_y, courant, tables, out, field, speed_x, speed_y, side, ring, table, flux,
                  todo, load_sem, row_sem, x_sem, y_sem, ring_sem, out_sem):
    me, lat = lax.axis_index("lon"), lax.axis_index("lat")
    clon, clat, nf = tracer.shape
    half = clon * 4
    blocks = -(-half // BLOCK)
    deep = ring.shape[0]
    wide = clon + 16
    top, bottom = lat > 0, lat < bands - 1
    lead = ROWS_AT_EDGE
    mid = pl.ds(8, clon)

    loads = [
        pltpu.make_async_copy(src, dst, load_sem.at[k])
        for k, (src, dst) in enumerate((
            (tables.at[me], table),
            (lon_low, side.at[pl.ds(0, 2)]),
            (lon_high, side.at[pl.ds(2, 2)]),
            (edge_x, side.at[pl.ds(4, 1)]),
            (lat_low.at[0], field.at[0, mid]),
            (lat_low.at[1], field.at[1, mid]),
            (lat_high.at[0], field.at[clat + 2, mid]),
            (lat_high.at[1], field.at[clat + 3, mid]),
            (edge_y.at[0], speed_y.at[clat]),
        ))
    ]
    for copy in loads:
        copy.start()

    def cells(row):
        return pltpu.make_async_copy(tracer.at[:, row, :], field.at[row + lead, mid], row_sem.at[row])

    def along(row):
        return pltpu.make_async_copy(courant.at[0, :, row, :], speed_x.at[row, pl.ds(0, clon)], x_sem.at[row])

    def across(row):
        return pltpu.make_async_copy(courant.at[1, :, row, :], speed_y.at[row], y_sem.at[row])

    def result(row):
        return pltpu.make_async_copy(field.at[row, mid], out.at[:, row, :], out_sem.at[row])

    @pl.loop(0, clat)
    def _(row):
        cells(row).start()

    def put(m, entry, place):
        row = lat * clat + entry - lead
        valid = (row >= 0) & (row < bands * clat)
        row = jnp.clip(row, 0, bands * clat - 1)
        low, count, padded = kept(cut_ref[row], half)
        polar = valid & (mask_ref[row] > 0)

        @pl.when(polar)
        def _():
            for b in range(blocks):
                todo[0, m + b] = place + b * BLOCK
                todo[1, m + b] = entry
                todo[2, m + b] = jnp.where(low, 0, blocks) + b
                todo[3, m + b] = count - b * BLOCK

        return (m + jnp.where(polar, (padded + BLOCK - 1) // BLOCK, 0), jnp.where(polar, padded, 0))

    m = jnp.int32(0)
    base = 2 * lead * half
    for k in range(2 * lead):
        m, _ = put(m, k if k < lead else clat + k, k * half)
    for k in range(2 * lead):
        m, _ = put(m, lead + k if k < lead else clat - lead + k, base + k * half)

    def listed(entry, carry):
        m, place = carry
        m, more = put(m, entry, place)
        return m, place + more

    m, _ = lax.fori_loop(2 * lead, clat, listed, (m, base + start_ref[0]))
    for u in range(UNROLL):
        todo[0, m + u] = 0
        todo[1, m + u] = clat + 2 * lead
        todo[2, m + u] = blocks
        todo[3, m + u] = 0
    rounds = (m + UNROLL - 1) // UNROLL

    def fetch(j):
        slot = lax.rem(j, deep)
        return pltpu.make_async_copy(
            totals.at[pl.ds(pl.multiple_of(todo[0, j], 8), BLOCK)], ring.at[slot], ring_sem.at[slot])

    ahead = deep // UNROLL - 1
    for k in range(ahead):
        @pl.when(k < rounds)
        def _(k=k):
            for u in range(UNROLL):
                fetch(k * UNROLL + u).start()

    @pl.loop(0, clat)
    def _(row):
        across(row).start()
        along(row).start()

    for copy in loads:
        copy.wait()

    @pl.loop(0, clat)
    def _(row):
        cells(row).wait()

    zero = jnp.zeros((clon, nf), jnp.float32)

    @pl.when(jnp.logical_not(top))
    def _():
        field[0, 8:8 + clon] = zero
        field[1, 8:8 + clon] = zero

    @pl.when(jnp.logical_not(bottom))
    def _():
        field[clat + 2, 8:8 + clon] = zero
        field[clat + 3, 8:8 + clon] = zero
        speed_y[clat] = zero

    flat = field.reshape((clat + 2 * lead + 1) * wide, nf)
    for k, lon in enumerate((6, 7, clon + 8, clon + 9)):
        flat[pl.ds(lead * wide + lon, clat, stride=wide), :] = side[k]
    index = lax.broadcasted_iota(jnp.int32, (BLOCK, nf), 0)

    @pl.loop(0, rounds)
    def _(k):
        @pl.when(k + ahead < rounds)
        def _():
            for u in range(UNROLL):
                fetch((k + ahead) * UNROLL + u).start()

        items = [k * UNROLL + u for u in range(UNROLL)]
        for j in items:
            fetch(j).wait()
        parts = []
        for j in items:
            s = jnp.where(index < todo[3, j], ring[lax.rem(j, deep)], 0.0)
            s = jnp.where(todo[2, j] < blocks, s, -s)
            high, rest = split(s)
            parts.append(jnp.dot(table[todo[2, j]], jnp.concatenate([high, high, rest], axis=0),
                                 preferred_element_type=jnp.float32))
        for j, value in zip(items, parts):
            row = todo[1, j]
            field[row] = jnp.where(todo[2, j] == 0, value, field[row] + value)

    @pl.loop(0, clat)
    def _(row):
        across(row).wait()
        along(row).wait()

    flat_x = speed_x.reshape(clat * (clon + 8), nf)
    flat_x[pl.ds(clon, clat, stride=clon + 8), :] = side[4]

    def flux_y(i):
        f = lambda k: field[i + k, 8:8 + clon, :]
        return speed_y[i] * limited(f(0), f(1), f(2), f(3))

    def row_step(r, low_flux):
        high_flux = flux_y(r + 1)
        f = lambda start, count: field[r + lead, start:start + count, :]
        value = f(8, clon)
        flux[0:clon] = speed_x[r, 0:clon] * limited(f(6, clon), f(7, clon), value, f(9, clon))
        flux[clon:clon + 1] = speed_x[r, clon:clon + 1] * limited(
            f(6 + clon, 1), f(7 + clon, 1), f(8 + clon, 1), f(9 + clon, 1))
        field[r, 8:8 + clon, :] = value - (flux[1:clon + 1] - flux[0:clon]) - (high_flux - low_flux)
        result(r).start()
        return high_flux

    lax.fori_loop(0, clat, row_step, flux_y(0))

    @pl.loop(0, clat)
    def _(row):
        result(row).wait()


def by_spectrum(tracer, courant, polar_mask, cutoff, which, start, devices, bands):
    clon, clat, nf = tracer.shape
    nlon = clon * devices
    half = nlon // 2
    most = 2 * LIMITS[-1][0]
    items = (clat + 2 * ROWS_AT_EDGE) * -(-half // BLOCK) + 2 * UNROLL
    smem = pl.BlockSpec(memory_space=pltpu.SMEM)
    hbm = pl.BlockSpec(memory_space=pltpu.HBM)
    dma = pltpu.SemaphoreType.DMA
    shape = lambda *dims: jax.ShapeDtypeStruct(dims, jnp.float32)
    big = pltpu.CompilerParams(vmem_limit_bytes=65000 << 10)
    forward, inverse = forward_tables(nlon, devices), inverse_tables(nlon, devices)

    packed = pl.pallas_call(
        forward_kernel,
        out_shape=shape((most + 1) * half, nf),
        in_specs=[smem] * 3 + [hbm] * 2,
        out_specs=hbm,
        scratch_shapes=[
            pltpu.VMEM((clat, clon, nf), jnp.float32), pltpu.VMEM(forward.shape[1:], jnp.bfloat16),
            pltpu.VMEM(((most + 1) * half, nf), jnp.float32),
            pltpu.SMEM((4, items), jnp.int32),
            dma((clat,)), dma, dma((most + 1,))],
        compiler_params=big,
        name="forward",
    )(polar_mask, cutoff, start, tracer, jnp.asarray(forward))

    def exchange(n, lent, which):
        chunk = half // 2
        buffer, less = [pltpu.VMEM((k, chunk, nf), jnp.float32) for k in (n, lent)]

        def call(start, packed, tracer, courant):
            return pl.pallas_call(
                functools.partial(exchange_kernel, bands),
                out_shape=(shape((most + 2 * 2 * ROWS_AT_EDGE) * half, nf), shape(2, clat, nf), shape(2, clat, nf),
                           shape(2, clon, nf), shape(2, clon, nf), shape(1, clat, nf), shape(1, clon, nf)),
                in_specs=[smem] + [hbm] * 3,
                out_specs=(hbm,) * 7,
                scratch_shapes=[buffer] * 4 + [less] * 2 + [dma((n,))] * 10 + [dma((lent,))] * 9
                + [dma((2 * ROWS_AT_EDGE, 2)), dma((2 * ROWS_AT_EDGE, 2)), dma((8,)), dma((8,))],
                compiler_params=pltpu.CompilerParams(
                    collective_id=1 + which, has_side_effects=True, vmem_limit_bytes=65000 << 10),
                name=f"exchange_{n}",
            )(start, packed, tracer, courant)

        return call

    parts = lax.switch(which, [exchange(n, lent, i) for i, (n, lent) in enumerate(LIMITS)], start, packed, tracer, courant)

    return pl.pallas_call(
        functools.partial(finish_kernel, bands),
        out_shape=shape(clon, clat, nf),
        in_specs=[smem] * 3 + [hbm] * 10,
        out_specs=hbm,
        scratch_shapes=[
            pltpu.VMEM((clat + 2 * ROWS_AT_EDGE + 1, clon + 16, nf), jnp.float32),
            pltpu.VMEM((clat, clon + 8, nf), jnp.float32), pltpu.VMEM((clat + 1, clon, nf), jnp.float32),
            pltpu.VMEM((5, clat, nf), jnp.float32),
            pltpu.VMEM((4 * UNROLL, BLOCK, nf), jnp.float32), pltpu.VMEM(inverse.shape[1:], jnp.bfloat16),
            pltpu.VMEM((clon + 8, nf), jnp.float32),
            pltpu.SMEM((4, items), jnp.int32),
            dma((9,)), dma((clat,)), dma((clat,)), dma((clat,)), dma((4 * UNROLL,)), dma((clat,))],
        compiler_params=big,
        name="finish",
    )(polar_mask, cutoff, start, parts[0], tracer, *parts[1:], courant, jnp.asarray(inverse))


def on_device(tracer, courant, polar_mask, cutoff):
    devices, bands = lax.axis_size("lon"), lax.axis_size("lat")
    clon, clat, _ = tracer.shape
    fits = clat % (8 * devices) == 0 and bands > 2

    def by_circles(tracer, courant, polar_mask, cutoff):
        build = by_kernel if fits else by_collectives
        parts = build(tracer, courant, polar_mask, cutoff, devices, bands)
        return advect(*parts, courant, bands)

    if not (fits and devices == 8 and bands == 4 and clon % 144 == 0):
        return by_circles(tracer, courant, polar_mask, cutoff)
    half = clon * devices // 2
    fixed = 2 * ROWS_AT_EDGE
    _, _, padded = kept(cutoff, half)
    padded = jnp.where(polar_mask > 0, padded, 0).reshape(bands, clat)[:, ROWS_AT_EDGE:clat - ROWS_AT_EDGE]
    sums = padded.sum(axis=1)
    lent = jnp.stack([sums[0], sums[3]])
    light = jnp.stack([sums[1], sums[2]])
    need = (jnp.max(jnp.maximum((lent + light + 1) // 2, light)) + half - 1) // half + fixed
    whole = (jnp.max(lent) + half - 1) // half + 2 * fixed
    which = len(LIMITS)
    size = 0
    for i, (n, more) in reversed(list(enumerate(LIMITS))):
        enough = (need <= n) & (whole <= n + more)
        which = jnp.where(enough, i, which)
        size = jnp.where(enough, n, size)
    lat = lax.axis_index("lat")
    helper = (lat == 1) | (lat == 2)
    start = jnp.where(helper, size * half - jnp.where(lat == 1, sums[1], sums[2]), fixed * half)
    return lax.cond(
        which < len(LIMITS),
        lambda *args: by_spectrum(*args, which, start.reshape(1), devices, bands),
        by_circles,
        tracer, courant, polar_mask, cutoff)


def solution(mesh):
    return jax.shard_map(
        on_device,
        mesh=mesh,
        in_specs=(P("lon", "lat", None), P(None, "lon", "lat", None), P(), P()),
        out_specs=P("lon", "lat", None),
        check_vma=False,
    )
```
